256 devices in a mesh: energy: 32 (over x, y, core), space: 8 (over z).
Axes of the slice: x: 4, y: 4, z: 8, core: 2. Of those that a mesh axis runs over, the one named last changes fastest.
Arguments:
- onsite: float32 [8, 2, 128, 128], P('space'), may hold values from -0.25 to 0.25
- hopping: float32 [8, 2, 128, 128], P('space'), may hold values from -0.25 to 0.25
- sigma_old: float32 [32, 8, 2, 128, 128], P('energy', 'space'), may hold values from -0.0390625 to 0.0390625
- screened: float32 [32, 8, 2, 3, 2, 128, 128], P('energy', 'space'), may hold values from -1 to 1
Outputs:
- green_retarded: float32 [32, 8, 3, 2, 128, 128], P('energy', 'space')
- self_energy: float32 [32, 8, 2, 3, 2, 128, 128], P('energy', 'space')
The draws below stay inside these ranges and needn't reach their ends.
All inputs are finite; a program needn't handle non-finite values.
Results may differ from the reference program's by a relative error of at most 0.0003.
Values sent between devices are 32-bit elements; how exact they have to be, the bound alone decides.
A program may use at most 128 MiB of HBM per device.

```python
import jax
import jax.numpy as jnp
from jax import lax

B = 128
NE = 32
NC = 8


def block_levels(stream_key, dims, cuts, smallest, high):
    gain, own = 1.0, jax.random.fold_in(stream_key, 6)
    for axis_at, blocks in cuts:
        draws = jnp.exp(jax.random.uniform(jax.random.fold_in(own, axis_at), (blocks,), jnp.float32, smallest / len(cuts), high / len(cuts)))
        gain = gain * jnp.repeat(draws, dims[axis_at] // blocks).reshape([-1 if axis == axis_at else 1 for axis in range(len(dims))])
    return gain


def noise(own_key, extent, deviation, reach, split=(), kind=jnp.bfloat16):
    result = jax.random.normal(own_key, extent, jnp.float32) * deviation
    if len(split) > 0:
        result = block_levels(own_key, extent, split, -0.22, 0.18) * result
    return jnp.clip(result, min=-reach, max=reach).astype(kind)


def setup_inputs(seed: int = 0) -> dict:
    splits = jax.random.split(jax.random.key(seed), 5)
    return {
        "onsite": noise(splits[0], (NC, 2, B, B), (B * 4) ** -0.5, 0.25, ((0, 8),), jnp.float32),
        "hopping": noise(splits[1], (NC, 2, B, B), (B * 4) ** -0.5, 0.25, ((0, 8),), jnp.float32),
        "sigma_old": noise(splits[2], (NE, NC, 2, B, B), (B * 200) ** -0.5, 0.0390625, ((0, 32), (1, 8)), jnp.float32),
        "screened": noise(splits[3], (NE, NC, 2, 3, 2, B, B), NE ** -0.5, 1.0, ((0, 32), (1, 8)), jnp.float32),
    }


BROADEN = 0.45
THERMAL = 0.1
PRECISE = lax.Precision.HIGHEST

def matmul_high(first, second):
    return jnp.matmul(first, second, precision=PRECISE)

def complex_product(first, second):
    real_part = matmul_high(first[0], second[0]) - matmul_high(first[1], second[1])
    imag_part = matmul_high(first[0], second[1]) + matmul_high(first[1], second[0])
    return jnp.stack([real_part, imag_part])

def dagger(blocks):
    return jnp.stack([jnp.swapaxes(blocks[0], -1, -2), -jnp.swapaxes(blocks[1], -1, -2)])

def invert_exact(blocks):
    size_order = blocks.shape[-1]
    upper_half = jnp.concatenate([blocks[0], -blocks[1]], axis=-1)
    lower_half = jnp.concatenate([blocks[1], blocks[0]], axis=-1)
    embedded = jnp.concatenate([upper_half, lower_half], axis=-2)
    target = jnp.concatenate([jnp.eye(size_order, dtype=blocks.dtype), jnp.zeros((size_order, size_order), blocks.dtype)], axis=0)
    target = jnp.broadcast_to(target, embedded.shape[:-1] + (size_order,))
    solved = jnp.linalg.solve(embedded, target)
    return jnp.stack([solved[..., :size_order, :], solved[..., size_order:, :]])

def convolve_cell(operands):
    green_cell, kernel_cell = operands
    energies_all = green_cell.shape[0]
    padded = jnp.concatenate([jnp.zeros_like(green_cell), green_cell], axis=0)

    def accumulate(running, offset):
        shifted = lax.dynamic_slice_in_dim(padded, (energies_all - offset).astype(jnp.int32), energies_all, 0)
        weight = kernel_cell[offset]
        real_part = shifted[:, :, :, 0] * weight[:, :, 0] - shifted[:, :, :, 1] * weight[:, :, 1]
        imag_part = shifted[:, :, :, 0] * weight[:, :, 1] + shifted[:, :, :, 1] * weight[:, :, 0]
        return (running + jnp.stack([real_part, imag_part], axis=3), None)
    running, _ = lax.scan(accumulate, jnp.zeros_like(green_cell), jnp.arange(energies_all, dtype=jnp.int32))
    return jnp.stack([-running[:, :, :, 1], running[:, :, :, 0]], axis=3)

def reference(onsite, hopping, sigma_old, screened):
    energies_all = sigma_old.shape[0]
    cells_all = sigma_old.shape[1]
    size_order = sigma_old.shape[-1]
    float_type = sigma_old.dtype
    energy = -1.5 + 3.0 * (jnp.arange(energies_all).astype(float_type) + 0.5) / energies_all
    identity = jnp.eye(size_order, dtype=float_type)
    magnitude = energy * energy + BROADEN * BROADEN
    contact = jnp.stack([(energy / magnitude)[:, None, None] * identity, (-BROADEN / magnitude)[:, None, None] * identity])
    systems = []
    for cell_index in range(cells_all):
        hamiltonian = 0.5 * (onsite[cell_index] + dagger(onsite[cell_index]))
        local_sigma = jnp.moveaxis(sigma_old[:, cell_index], 1, 0)
        systems.append(jnp.stack([energy[:, None, None] * identity - hamiltonian[0] - local_sigma[0], BROADEN * identity - hamiltonian[1] - local_sigma[1]]))
    couplings = [hopping[cell_index] for cell_index in range(cells_all)] + [jnp.zeros_like(hopping[0])]
    left_previous = []
    previous = contact
    for cell_index in range(cells_all):
        left_previous.append(previous)
        coupling = couplings[cell_index]
        previous = invert_exact(systems[cell_index] - complex_product(dagger(coupling), complex_product(previous, coupling)))
    right_following = [None] * cells_all
    following = jnp.zeros_like(contact)
    for cell_index in reversed(range(cells_all)):
        right_following[cell_index] = following
        ahead_coupling = couplings[cell_index + 1]
        following = invert_exact(systems[cell_index] - complex_product(ahead_coupling, complex_product(following, dagger(ahead_coupling))))
    occupation = 1.0 / (1.0 + jnp.exp(energy / THERMAL))
    occupied = occupation[None, :, None, None, None]
    greens = []
    kinds = []
    for cell_index in range(cells_all):
        coupling = couplings[cell_index]
        ahead_coupling = couplings[cell_index + 1]
        self_left = complex_product(dagger(coupling), complex_product(left_previous[cell_index], coupling))
        self_right = complex_product(ahead_coupling, complex_product(right_following[cell_index], dagger(ahead_coupling)))
        diagonal = invert_exact(systems[cell_index] - self_left - self_right)
        upper_block = complex_product(left_previous[cell_index], complex_product(coupling, diagonal))
        lower_block = complex_product(diagonal, complex_product(dagger(coupling), left_previous[cell_index]))
        stacked = jnp.stack([diagonal, upper_block, lower_block], axis=2)
        spectral = jnp.stack([diagonal - dagger(diagonal), upper_block - dagger(lower_block), lower_block - dagger(upper_block)], axis=2)
        both_kinds = jnp.stack([-occupied * spectral, (1.0 - occupied) * spectral])
        greens.append(jnp.transpose(stacked, (1, 2, 0, 3, 4)))
        kinds.append(jnp.transpose(both_kinds, (2, 0, 3, 1, 4, 5)))
    green_retarded = jnp.stack(greens, axis=1)
    lesser_greater = jnp.stack(kinds, axis=0)
    kernel = jnp.moveaxis(screened, 1, 0)
    sigma_cells = lax.map(convolve_cell, (lesser_greater, kernel))
    return (green_retarded, jnp.moveaxis(sigma_cells, 0, 1))
```

```python
import jax
import jax.numpy as jnp
from jax import lax
from jax.experimental import pallas as pl
from jax.experimental.pallas import tpu as pltpu
from jax.sharding import PartitionSpec as P

BROADEN = 0.45
THERMAL = 0.1
B = 128
NE = 32
NC = 8
PANEL = 16
MESH = pl.DeviceIdType.MESH
F32 = jnp.float32


def split(x):
    high = x.astype(jnp.bfloat16)
    return high, (x - high.astype(F32)).astype(jnp.bfloat16)


def dot(a, b):
    return lax.dot_general(a, b, (((1,), (0,)), ((), ())), preferred_element_type=F32)


def product(xr, xi, yr, yi):
    left = jnp.concatenate([xr, xi], axis=1)
    right = jnp.concatenate(
        [jnp.concatenate([yr, yi], axis=1), jnp.concatenate([-yi, yr], axis=1)], axis=0
    )
    lh, ll = split(left)
    rh, rl = split(right)
    out = dot(lh, rh) + (dot(lh, rl) + dot(ll, rh))
    return out[:, :B], out[:, B:]


def mm(x, y):
    return product(x[0], x[1], y[0], y[1])


def put(ref, pair):
    ref[0] = pair[0]
    ref[1] = pair[1]


def put_dagger(ref, x):
    ref[0] = x[0].T
    ref[1] = -x[1].T


def tile_inverse(tr, ti, off, lane, sub):
    shape = tr.shape
    cols = [
        (
            jnp.broadcast_to(tr[:, off + j : off + j + 1], shape),
            jnp.broadcast_to(ti[:, off + j : off + j + 1], shape),
        )
        for j in range(8)
    ]
    for k in range(8):
        cr, ci = cols[k]
        pr = jnp.broadcast_to(cr[k : k + 1], shape)
        pi = jnp.broadcast_to(ci[k : k + 1], shape)
        inv = 1.0 / (pr * pr + pi * pi)
        qr = pr * inv
        qi = -(pi * inv)
        own = sub == k
        mr = jnp.where(own, -qr, cr * qr - ci * qi)
        mi = jnp.where(own, -qi, cr * qi + ci * qr)

        def step(xr, xi):
            br = jnp.broadcast_to(xr[k : k + 1], shape)
            bi = jnp.broadcast_to(xi[k : k + 1], shape)
            return (
                jnp.where(own, 0.0, xr) - (mr * br - mi * bi),
                jnp.where(own, 0.0, xi) - (mr * bi + mi * br),
            )

        for j in range(k + 1, 8):
            cols[j] = step(*cols[j])
        here = lane == off + k
        tr, ti = step(
            jnp.where(here, jnp.where(own, 1.0, 0.0), tr), jnp.where(here, 0.0, ti)
        )
    return tr, ti


def panel_inverse(pr, pi):
    shape = (8, B)
    lane = lax.broadcasted_iota(jnp.int32, shape, 1)
    sub = lax.broadcasted_iota(jnp.int32, shape, 0)
    tiles = [(pr[8 * t : 8 * t + 8], pi[8 * t : 8 * t + 8]) for t in range(PANEL // 8)]
    for t in range(len(tiles)):
        off = 8 * t
        tiles[t] = tile_inverse(*tiles[t], off, lane, sub)
        tr, ti = tiles[t]
        active = (lane >= off) & (lane < off + 8)
        for u in range(len(tiles)):
            if u == t:
                continue
            xr, xi = tiles[u]
            sr, si = jnp.zeros(shape, F32), jnp.zeros(shape, F32)
            for j in range(8):
                cr = jnp.broadcast_to(xr[:, off + j : off + j + 1], shape)
                ci = jnp.broadcast_to(xi[:, off + j : off + j + 1], shape)
                rr = jnp.broadcast_to(tr[j : j + 1], shape)
                ri = jnp.broadcast_to(ti[j : j + 1], shape)
                sr = sr + (cr * rr - ci * ri)
                si = si + (cr * ri + ci * rr)
            tiles[u] = (jnp.where(active, 0.0, xr) - sr, jnp.where(active, 0.0, xi) - si)
    return jnp.concatenate([x[0] for x in tiles]), jnp.concatenate([x[1] for x in tiles])


def invert(x):
    rest, back = B - PANEL, B - PANEL
    lane = lax.broadcasted_iota(jnp.int32, (rest, B), 1)

    def body(_, panel):
        xr, xi = x[0, PANEL:, :], x[1, PANEL:, :]
        columns = jnp.concatenate([xr[:, :PANEL], xi[:, :PANEL]], axis=1)
        ch, cl = split(columns)
        x[0, :rest, :] = pltpu.roll(jnp.where(lane < PANEL, 0.0, xr), back, 1)
        x[1, :rest, :] = pltpu.roll(jnp.where(lane < PANEL, 0.0, xi), back, 1)
        rr, ri = panel_inverse(*panel)
        rr, ri = pltpu.roll(rr, back, 1), pltpu.roll(ri, back, 1)
        rows = jnp.concatenate(
            [jnp.concatenate([rr, ri], axis=1), jnp.concatenate([-ri, rr], axis=1)], axis=0
        )
        rh, rl = split(rows)
        update = dot(
            jnp.concatenate([ch, ch, cl], axis=1), jnp.concatenate([rh, rl, rh], axis=0)
        )
        nr = x[0, :rest, :] - update[:, :B]
        ni = x[1, :rest, :] - update[:, B:]
        x[0, :rest, :] = nr
        x[1, :rest, :] = ni
        x[0, rest:, :] = rr
        x[1, rest:, :] = ri
        return nr[:PANEL], ni[:PANEL]

    lax.fori_loop(0, B // PANEL, body, (x[0, :PANEL, :], x[1, :PANEL, :]))


def kernel(
    onsite, hopping, sigma, screened, green, out,
    ahead, arrived, middle, outer, x, m, k1, k1h, k2, k2h, t, v, p, q2,
    spectral, wbuf, dbuf, scaled, factor, sbuf,
    s_hop, s_chain, s_mid, s_out, s_w, s_d, s_relay, s_sig,
    r_hop, r_chain, r_mid, r_out, r_w, r_d, r_relay, r_sig,
):
    e = lax.axis_index("energy")
    j = lax.axis_index("space")
    chip, core = e // 2, e % 2
    cx, cy = chip // 4, chip % 4
    left = j < NC // 2
    is_mid = (j == NC // 2 - 1) | (j == NC // 2)
    row = pl.multiple_of(chip * 8, 8)

    def relative(i):
        return ((cx + i // 4) % 4) * 4 + (cy + i % 4) % 4

    barrier = pltpu.get_barrier_semaphore()

    def greet(i, c):
        pl.semaphore_signal(
            barrier, inc=1, device_id={"energy": (e + i) % NE}, device_id_type=MESH
        )
        return c

    for step in (1, NC - 1):
        pl.semaphore_signal(
            barrier, inc=1, device_id={"space": (j + step) % NC}, device_id_type=MESH
        )
    lax.fori_loop(1, NE, greet, 0)

    def energy_of(n, shape):
        return -1.5 + 3.0 * (jnp.full(shape, n, jnp.int32).astype(F32) + 0.5) / NE

    eye = lax.broadcasted_iota(jnp.int32, (B, B), 0) == lax.broadcasted_iota(
        jnp.int32, (B, B), 1
    )
    en = energy_of(e, (B, B))
    on_r, on_i = onsite[0, 0], onsite[0, 1]
    m[0] = jnp.where(eye, en, 0.0) - 0.5 * (on_r + on_r.T) - sigma[0, 0, 0]
    m[1] = jnp.where(eye, BROADEN, 0.0) - 0.5 * (on_i - on_i.T) - sigma[0, 0, 1]
    hop = hopping.at[0]

    @pl.when(left)
    def _():
        put(k1, hop)
        put_dagger(k1h, hop)

    @pl.when(jnp.logical_not(left))
    def _():
        put(k2h, hop)
        put_dagger(k2, hop)

    @pl.when(j == 0)
    def _():
        size = en * en + BROADEN * BROADEN
        arrived[0] = jnp.where(eye, en / size, 0.0)
        arrived[1] = jnp.where(eye, -BROADEN / size, 0.0)

    @pl.when(j == NC - 1)
    def _():
        for ref in (arrived, k1, k1h):
            ref[...] = jnp.zeros_like(ref)

    pl.semaphore_wait(barrier, NE - 1 + 2)

    def to_space(src, dst, s, r, where):
        return pltpu.make_async_remote_copy(
            src_ref=src, dst_ref=dst, send_sem=s, recv_sem=r,
            device_id={"space": where}, device_id_type=MESH,
        )

    def to_energy(src, dst, s, r, where):
        return pltpu.make_async_remote_copy(
            src_ref=src, dst_ref=dst, send_sem=s, recv_sem=r,
            device_id={"energy": where}, device_id_type=MESH,
        )

    down = jnp.maximum(j - 1, 0)
    up = jnp.minimum(j + 1, NC - 1)
    inner = jnp.where(left, up, down)
    outward = jnp.where(left, down, up)
    hop_copy = to_space(hop, ahead, s_hop, r_hop, down)

    @pl.when(j > 0)
    def _():
        hop_copy.start()

    def send_w(i, c):
        other = relative(i // 2)
        kind = (core + i % 2) % 2
        to_energy(
            screened.at[0, 0, kind, :, :, pl.ds(pl.multiple_of(other * 8, 8), 8), :],
            wbuf.at[e], s_w, r_w, other * 2 + kind,
        ).start()
        return c

    lax.fori_loop(1, NE, send_w, 0)
    wbuf[e] = screened[0, 0, core, :, :, pl.ds(row, 8), :]

    @pl.when(jnp.logical_not(left) & (j < NC - 1))
    def _():
        hop_copy.wait_recv()
        put(k1h, ahead)
        put_dagger(k1, ahead)

    def occupations(n, c):
        f = 1.0 / (1.0 + jnp.exp(energy_of(n, (8, B)) / THERMAL))
        factor[n] = jnp.where(jnp.full((8, B), core, jnp.int32) == 0, -f, 1.0 - f)
        return c

    chain = to_space(x, arrived, s_chain, r_chain, inner)
    meet = to_space(x, middle, s_mid, r_mid, inner)

    @pl.when((j > 0) & (j < NC - 1))
    def _():
        chain.wait_recv()

    put(t, mm(k1h, arrived))
    sr, si = mm(t, k1)
    m[0] = m[0] - sr
    m[1] = m[1] - si
    x[...] = m[...]
    invert(x)

    @pl.when(jnp.logical_not(is_mid))
    def _():
        chain.start()

    @pl.when(is_mid)
    def _():
        meet.start()

    lax.fori_loop(0, NE, occupations, 0)
    for n in range(8):
        scaled[n] = jnp.zeros_like(scaled[n])

    @pl.when(left)
    def _():
        hop_copy.wait_recv()
        put(k2, ahead)
        put_dagger(k2h, ahead)
        put(v, mm(arrived, k1))

    g = green.at[0, 0, 0]
    onward = to_space(g, outer, s_out, r_out, outward)

    @pl.when(is_mid)
    def _():
        meet.wait_recv()
        ar, ai = mm(k2, middle)
        sr, si = product(ar, ai, k2h[0], k2h[1])
        g[0] = m[0] - sr
        g[1] = m[1] - si
        invert(g)
        onward.start()

        @pl.when(j == NC // 2)
        def _():
            put(t, (ar, ai))
            put(v, mm(middle, k2h))

    @pl.when(jnp.logical_not(is_mid))
    def _():
        put(p, mm(x, k2))
        put(q2, mm(k2h, x))
        onward.wait_recv()
        put(m, mm(p, outer))
        ar, ai = mm(m, q2)
        g[0] = x[0] + ar
        g[1] = x[1] + ai

        @pl.when((j > 0) & (j < NC - 1))
        def _():
            onward.start()

    @pl.when(j <= NC // 2)
    def _():
        put(green.at[0, 0, 1], mm(v, g))
        put(green.at[0, 0, 2], mm(g, t))

    @pl.when(j > NC // 2)
    def _():
        put(green.at[0, 0, 1], mm(outer, q2))
        put(green.at[0, 0, 2], (m[0], m[1]))

    u, w = green.at[0, 0, 1], green.at[0, 0, 2]
    spectral[0, 0] = g[0] - g[0].T
    spectral[0, 1] = g[1] + g[1].T
    dr = u[0] - w[0].T
    di = u[1] + w[1].T
    spectral[1, 0] = dr
    spectral[1, 1] = di
    spectral[2, 0] = -dr.T
    spectral[2, 1] = di.T

    def send_d(i, c):
        other = relative(i)
        to_energy(
            spectral.at[:, :, pl.ds(pl.multiple_of(other * 8, 8), 8), :],
            dbuf.at[core, chip], s_d, r_d, other * 2 + core,
        ).start()
        return c

    lax.fori_loop(1, NE // 2, send_d, 0)
    dbuf[core, chip] = spectral[:, :, pl.ds(row, 8), :]
    some = dbuf.at[0, pl.ds(0, NE // 2 - 1)]
    to_energy(some, some, s_d, r_d, e).wait_recv()
    relay = to_energy(dbuf.at[core], dbuf.at[core], s_relay, r_relay, chip * 2 + 1 - core)
    relay.start()
    many = wbuf.at[pl.ds(0, NE - 1)]
    to_energy(many, many, s_w, r_w, e).wait_recv()
    relay.wait_recv()

    def scale(n, c):
        scaled[8 + n] = dbuf[n % 2, n // 2] * factor[n]
        return c

    lax.fori_loop(0, NE, scale, 0)

    def convolve(turn, c):
        start = ((cx + turn) % 4) * 8
        for b in range(3):
            zero = jnp.zeros((8, B), F32)

            def add(k, acc):
                wr, wi = wbuf[k, b, 0], wbuf[k, b, 1]
                new = []
                for i in range(8):
                    lr = scaled[8 + start + i - k, b, 0]
                    li = scaled[8 + start + i - k, b, 1]
                    ar, ai = acc[i]
                    new.append((ar + (lr * wr - li * wi), ai + (lr * wi + li * wr)))
                return tuple(new)

            def add8(k, acc):
                for s in range(8):
                    acc = add(k * 8 + s, acc)
                return acc

            acc = lax.fori_loop(0, start // 8 + 1, add8, tuple((zero, zero) for _ in range(8)))
            for i in range(8):
                sbuf[start + i, b, 0] = -acc[i][1]
                sbuf[start + i, b, 1] = acc[i][0]

        def send_s(i, c2):
            n = start + (i + 2 * cy) % 8

            @pl.when(n != e)
            def _():
                to_energy(
                    sbuf.at[n], out.at[0, 0, core, :, :, pl.ds(row, 8), :], s_sig, r_sig, n
                ).start()

            return c2

        lax.fori_loop(0, 8, send_s, 0)
        return c

    lax.fori_loop(0, 4, convolve, 0)
    out[0, 0, core, :, :, pl.ds(row, 8), :] = sbuf[e]

    @pl.when(j > 0)
    def _():
        hop_copy.wait_send()

    @pl.when(jnp.logical_not(is_mid))
    def _():
        chain.wait_send()

    @pl.when(is_mid)
    def _():
        meet.wait_send()

    @pl.when((j > 0) & (j < NC - 1))
    def _():
        onward.wait_send()

    to_energy(many, many, s_w, r_w, e).wait_send()
    to_energy(some, some, s_d, r_d, e).wait_send()
    relay.wait_send()
    to_energy(many, many, s_sig, r_sig, e).wait_send()
    to_energy(many, many, s_sig, r_sig, e).wait_recv()


def local(onsite, hopping, sigma_old, screened):
    vmem = pl.BlockSpec(memory_space=pltpu.VMEM)
    square = pltpu.VMEM((2, B, B), F32)
    return pl.pallas_call(
        kernel,
        out_shape=(
            jax.ShapeDtypeStruct((1, 1, 3, 2, B, B), F32),
            jax.ShapeDtypeStruct((1, 1, 2, 3, 2, B, B), F32),
        ),
        in_specs=[vmem] * 4,
        out_specs=(vmem, vmem),
        scratch_shapes=[square] * 14
        + [
            pltpu.VMEM((3, 2, B, B), F32),
            pltpu.VMEM((NE, 3, 2, 8, B), F32),
            pltpu.VMEM((2, NE // 2, 3, 2, 8, B), F32),
            pltpu.VMEM((NE + 8, 3, 2, 8, B), F32),
            pltpu.VMEM((NE, 8, B), F32),
            pltpu.VMEM((NE, 3, 2, 8, B), F32),
        ]
        + [pltpu.SemaphoreType.DMA] * 16,
        compiler_params=pltpu.CompilerParams(
            collective_id=0, has_side_effects=True, vmem_limit_bytes=48 * 2**20
        ),
        name="transport",
    )(onsite, hopping, sigma_old, screened)


def solution(mesh):
    placed = (
        P("space", None, None, None),
        P("space", None, None, None),
        P("energy", "space", None, None, None),
        P("energy", "space", None, None, None, None, None),
    )
    return jax.shard_map(
        local,
        mesh=mesh,
        in_specs=placed,
        out_specs=(
            P("energy", "space", None, None, None, None),
            P("energy", "space", None, None, None, None, None),
        ),
        check_vma=False,
    )
```

```python
import jax
import jax.numpy as jnp
from jax import lax
from jax.experimental import pallas as pl
from jax.experimental.pallas import tpu as pltpu
from jax.sharding import PartitionSpec as P

BROADEN = 0.45
THERMAL = 0.1
B = 128
NE = 32
NC = 8
PANEL = 16
MESH = pl.DeviceIdType.MESH
F32 = jnp.float32


def split(x):
    high = x.astype(jnp.bfloat16)
    return high, (x - high.astype(F32)).astype(jnp.bfloat16)


def dot(a, b):
    return lax.dot_general(a, b, (((1,), (0,)), ((), ())), preferred_element_type=F32)


def product(xr, xi, yr, yi):
    left = jnp.concatenate([xr, xi], axis=1)
    right = jnp.concatenate(
        [jnp.concatenate([yr, yi], axis=1), jnp.concatenate([-yi, yr], axis=1)], axis=0
    )
    lh, ll = split(left)
    rh, rl = split(right)
    out = dot(lh, rh) + (dot(lh, rl) + dot(ll, rh))
    return out[:, :B], out[:, B:]


def mm(x, y):
    return product(x[0], x[1], y[0], y[1])


def put(ref, pair):
    ref[0] = pair[0]
    ref[1] = pair[1]


def put_dagger(ref, x):
    ref[0] = x[0].T
    ref[1] = -x[1].T


def tile_inverse(tr, ti, off, lane, sub):
    shape = tr.shape
    cols = [
        (
            jnp.broadcast_to(tr[:, off + j : off + j + 1], shape),
            jnp.broadcast_to(ti[:, off + j : off + j + 1], shape),
        )
        for j in range(8)
    ]
    for k in range(8):
        cr, ci = cols[k]
        pr = jnp.broadcast_to(cr[k : k + 1], shape)
        pi = jnp.broadcast_to(ci[k : k + 1], shape)
        inv = 1.0 / (pr * pr + pi * pi)
        qr = pr * inv
        qi = -(pi * inv)
        own = sub == k
        mr = jnp.where(own, -qr, cr * qr - ci * qi)
        mi = jnp.where(own, -qi, cr * qi + ci * qr)

        def step(xr, xi):
            br = jnp.broadcast_to(xr[k : k + 1], shape)
            bi = jnp.broadcast_to(xi[k : k + 1], shape)
            return (
                jnp.where(own, 0.0, xr) - (mr * br - mi * bi),
                jnp.where(own, 0.0, xi) - (mr * bi + mi * br),
            )

        for j in range(k + 1, 8):
            cols[j] = step(*cols[j])
        here = lane == off + k
        tr, ti = step(
            jnp.where(here, jnp.where(own, 1.0, 0.0), tr), jnp.where(here, 0.0, ti)
        )
    return tr, ti


def panel_inverse(pr, pi):
    shape = (8, B)
    lane = lax.broadcasted_iota(jnp.int32, shape, 1)
    sub = lax.broadcasted_iota(jnp.int32, shape, 0)
    tiles = [(pr[8 * t : 8 * t + 8], pi[8 * t : 8 * t + 8]) for t in range(PANEL // 8)]
    for t in range(len(tiles)):
        off = 8 * t
        tiles[t] = tile_inverse(*tiles[t], off, lane, sub)
        tr, ti = tiles[t]
        active = (lane >= off) & (lane < off + 8)
        for u in range(len(tiles)):
            if u == t:
                continue
            xr, xi = tiles[u]
            sr, si = jnp.zeros(shape, F32), jnp.zeros(shape, F32)
            for j in range(8):
                cr = jnp.broadcast_to(xr[:, off + j : off + j + 1], shape)
                ci = jnp.broadcast_to(xi[:, off + j : off + j + 1], shape)
                rr = jnp.broadcast_to(tr[j : j + 1], shape)
                ri = jnp.broadcast_to(ti[j : j + 1], shape)
                sr = sr + (cr * rr - ci * ri)
                si = si + (cr * ri + ci * rr)
            tiles[u] = (jnp.where(active, 0.0, xr) - sr, jnp.where(active, 0.0, xi) - si)
    return jnp.concatenate([x[0] for x in tiles]), jnp.concatenate([x[1] for x in tiles])


def invert(x):
    rest, back = B - PANEL, B - PANEL
    lane = lax.broadcasted_iota(jnp.int32, (rest, B), 1)

    def body(_, panel):
        xr, xi = x[0, PANEL:, :], x[1, PANEL:, :]
        columns = jnp.concatenate([xr[:, :PANEL], xi[:, :PANEL]], axis=1)
        ch, cl = split(columns)
        x[0, :rest, :] = pltpu.roll(jnp.where(lane < PANEL, 0.0, xr), back, 1)
        x[1, :rest, :] = pltpu.roll(jnp.where(lane < PANEL, 0.0, xi), back, 1)
        rr, ri = panel_inverse(*panel)
        rr, ri = pltpu.roll(rr, back, 1), pltpu.roll(ri, back, 1)
        rows = jnp.concatenate(
            [jnp.concatenate([rr, ri], axis=1), jnp.concatenate([-ri, rr], axis=1)], axis=0
        )
        rh, rl = split(rows)
        update = dot(
            jnp.concatenate([ch, ch, cl], axis=1), jnp.concatenate([rh, rl, rh], axis=0)
        )
        nr = x[0, :rest, :] - update[:, :B]
        ni = x[1, :rest, :] - update[:, B:]
        x[0, :rest, :] = nr
        x[1, :rest, :] = ni
        x[0, rest:, :] = rr
        x[1, rest:, :] = ri
        return nr[:PANEL], ni[:PANEL]

    lax.fori_loop(0, B // PANEL, body, (x[0, :PANEL, :], x[1, :PANEL, :]))


def kernel(
    onsite, hopping, sigma, screened, green, out,
    raw, c1, c1h, c2, c2h, c3, c3h, c4, c4h,
    m, x, r, y, v, t, k, kp, w1, w1p, f, fp, base, pa, pb,
    b_g0, b_g1, b_g2, b_a3, b_mo, b_k, b_kp, b_r, b_z,
    spectral, wbuf, dbuf, scaled, factor, sbuf,
    s_mat, s_w, s_d, s_relay, s_sig,
    r_raw, r_mat, r_w, r_d, r_relay, r_sig,
):
    e = lax.axis_index("energy")
    j = lax.axis_index("space")
    chip, core = e // 2, e % 2
    cx, cy = chip // 4, chip % 4
    left = j < NC // 2
    right = jnp.logical_not(left)
    place = jnp.where(left, j, NC - 1 - j)
    own = jnp.where(left, j, NC - j)
    row = pl.multiple_of(chip * 8, 8)

    def at(p):
        return jnp.where(left, p, NC - 1 - p)

    def relative(i):
        return ((cx + i // 4) % 4) * 4 + (cy + i % 4) % 4

    barrier = pltpu.get_barrier_semaphore()

    def greet_z(i, c):
        pl.semaphore_signal(
            barrier, inc=1, device_id={"space": (j + i) % NC}, device_id_type=MESH
        )
        return c

    def greet(i, c):
        pl.semaphore_signal(
            barrier, inc=1, device_id={"energy": (e + i) % NE}, device_id_type=MESH
        )
        return c

    lax.fori_loop(1, NC, greet_z, 0)
    lax.fori_loop(1, NE, greet, 0)

    def energy_of(n, shape):
        return -1.5 + 3.0 * (jnp.full(shape, n, jnp.int32).astype(F32) + 0.5) / NE

    eye = lax.broadcasted_iota(jnp.int32, (B, B), 0) == lax.broadcasted_iota(
        jnp.int32, (B, B), 1
    )
    en = energy_of(e, (B, B))
    on_r, on_i = onsite[0, 0], onsite[0, 1]
    m[0] = jnp.where(eye, en, 0.0) - 0.5 * (on_r + on_r.T) - sigma[0, 0, 0]
    m[1] = jnp.where(eye, BROADEN, 0.0) - 0.5 * (on_i - on_i.T) - sigma[0, 0, 1]
    hop = hopping.at[0]
    g, u, w = green.at[0, 0, 0], green.at[0, 0, 1], green.at[0, 0, 2]
    first = (place == 0) | (place == 2)

    def to_space(src, dst, s, r, where):
        return pltpu.make_async_remote_copy(
            src_ref=src, dst_ref=dst, send_sem=s, recv_sem=r,
            device_id={"space": where}, device_id_type=MESH,
        )

    def to_energy(src, dst, s, r, where):
        return pltpu.make_async_remote_copy(
            src_ref=src, dst_ref=dst, send_sem=s, recv_sem=r,
            device_id={"energy": where}, device_id_type=MESH,
        )

    pending = []

    def send(cond, src, dst, sem, where):
        copy = to_space(src, dst, s_mat.at[len(pending)], r_mat.at[sem], where)
        pending.append((cond, copy))
        pl.when(cond)(copy.start)

    def send_raw(cond, src, slot, where):
        copy = to_space(src, raw.at[slot], s_mat.at[len(pending)], r_raw.at[slot], where)
        pending.append((cond, copy))
        pl.when(cond)(copy.start)

    def have(ref, sem):
        to_space(ref, ref, s_mat.at[0], r_mat.at[sem], j).wait_recv()

    def have_raw(slot):
        ref = raw.at[slot]
        to_space(ref, ref, s_mat.at[0], r_raw.at[slot], j).wait_recv()

    def coupling(c, ch, x):
        xr, xi = x[0], x[1]
        dr, di = xr.T, -xi.T
        put(c, (jnp.where(left, xr, dr), jnp.where(left, xi, di)))
        put(ch, (jnp.where(left, dr, xr), jnp.where(left, di, xi)))

    def plus(a, b):
        return a[0] + b[0], a[1] + b[1]

    def minus(a, b):
        return a[0] - b[0], a[1] - b[1]

    pl.semaphore_wait(barrier, NE - 1 + NC - 1)

    send_raw(left & (place == 1), hop, 1, 0)
    send_raw(left & (place == 2), hop, 2, 1)
    send_raw(left & (place == 3), hop, 3, 1)
    send_raw(right & (place == 0), hop, 1, NC - 2)
    send_raw(right & (place == 1), hop, 2, NC - 3)
    send_raw(right & (place == 2), hop, 3, NC - 2)
    send_raw(left & (place == 2), hop, 2, 3)
    send_raw(left & (place == 3), hop, 3, 2)
    send_raw(right & (place == 3), hop, 4, 3)

    @pl.when(left & (place == 0))
    def _():
        size = en * en + BROADEN * BROADEN
        zr, zi = en / size, -BROADEN / size
        hr, hi = hop[0], hop[1]
        put(v, (zr * hr - zi * hi, zr * hi + zi * hr))
        hr, hi = hop[0].T, -hop[1].T
        put(t, (zr * hr - zi * hi, zr * hi + zi * hr))
        put(m, minus(m, mm(t, hop)))

    @pl.when(first)
    def _():
        x[...] = m[...]
        invert(x)

    send(place == 0, x, b_g0, 0, at(1))
    send(place == 2, x, b_g2, 2, at(1))
    send(place == 2, x, b_g2, 2, at(3))

    def send_w(i, c):
        other = relative(i // 2)
        kind = (core + i % 2) % 2
        to_energy(
            screened.at[0, 0, kind, :, :, pl.ds(pl.multiple_of(other * 8, 8), 8), :],
            wbuf.at[e], s_w, r_w, other * 2 + kind,
        ).start()
        return c

    lax.fori_loop(1, NE, send_w, 0)
    wbuf[e] = screened[0, 0, core, :, :, pl.ds(row, 8), :]

    def occupations(n, c):
        f = 1.0 / (1.0 + jnp.exp(energy_of(n, (8, B)) / THERMAL))
        factor[n] = jnp.where(jnp.full((8, B), core, jnp.int32) == 0, -f, 1.0 - f)
        return c

    @pl.when(place != 1)
    def _():
        lax.fori_loop(0, NE, occupations, 0)
        for n in range(8):
            scaled[n] = jnp.zeros_like(scaled[n])

    @pl.when(place == 3)
    def _():
        have(b_g2, 2)

    @pl.when(left & (place == 3))
    def _():
        have_raw(4)

    send(place == 3, m, b_a3, 3, at(1))
    send_raw(left & (place == 3), raw.at[4], 4, 1)
    send_raw(right & (place == 3), hop, 4, NC - 2)

    @pl.when(place == 1)
    def _():
        @pl.when(left)
        def _():
            coupling(c1, c1h, hop)
            have_raw(2)
            coupling(c2, c2h, raw.at[2])

        @pl.when(right)
        def _():
            coupling(c2, c2h, hop)
            have_raw(1)
            coupling(c1, c1h, raw.at[1])

        lax.fori_loop(0, NE, occupations, 0)
        for n in range(8):
            scaled[n] = jnp.zeros_like(scaled[n])
        have_raw(3)
        coupling(c3, c3h, raw.at[3])
        have(b_g2, 2)
        put(pa, mm(b_g2, c3))
        put(k, mm(c2, pa))
        put(kp, mm(c3h, b_g2))
        put(kp, mm(kp, c2h))
        put(base, mm(c3h, pa))
        put(pb, mm(c2, b_g2))
        put(m, minus(m, mm(pb, c2h)))
        have(b_g0, 0)
        put(t, mm(c1h, b_g0))
        put(m, minus(m, mm(t, c1)))

    send(place == 1, k, b_k, 5, at(0))
    send(place == 1, kp, b_kp, 6, at(0))

    @pl.when(place == 1)
    def _():
        x[...] = m[...]
        invert(x)
        put(w1, mm(x, k))
        put(y, mm(kp, w1))
        have(b_a3, 3)
        put(r, minus(minus(b_a3, base), y))
        m[...] = r[...]

    send(place == 1, m, b_mo, 4, NC - 1 - j)
    send(place == 1, x, b_g1, 1, at(2))
    send(left & (place == 1), x, b_g1, 1, 3)
    send(place == 1, x, b_g1, 1, at(0))

    @pl.when(place == 1)
    def _():
        invert(r)

    send(right & (place == 1), r, b_r, 7, NC // 2)

    @pl.when(place == 1)
    def _():
        have_raw(4)
        coupling(c4, c4h, raw.at[4])
        put(pa, mm(r, c4))
        put(pb, mm(c4h, pa))
        put(base, mm(c4h, r))
        have(b_mo, 4)
        put(y, minus(b_mo, pb))
        invert(y)

    send(right & (place == 1), y, b_z, 8, NC // 2)

    @pl.when(place == 1)
    def _():
        put(pb, mm(pa, y))
        put(b_z, plus(r, mm(pb, base)))

    send(left & (place == 1), b_z, b_z, 8, 3)
    send(place == 1, b_z, b_z, 8, at(2))
    send(place == 1, b_z, b_z, 8, at(0))

    @pl.when(place == 1)
    def _():
        put(w1p, mm(kp, x))
        put(f, mm(w1, b_z))
        put(g, plus(x, mm(f, w1p)))

        @pl.when(left)
        def _():
            put(v, mm(b_g0, c1))
            put(u, mm(v, g))
            put(w, mm(g, t))

        @pl.when(right)
        def _():
            put(pa, mm(b_z, w1p))
            put(pa, plus(mm(c2h, g), mm(c3, pa)))
            put(u, mm(b_g2, pa))
            put(pb, plus(mm(g, c2), mm(f, c3h)))
            put(w, mm(pb, b_g2))

    @pl.when(place == 0)
    def _():
        @pl.when(left)
        def _():
            have_raw(1)
            coupling(c1, c1h, raw.at[1])

        @pl.when(right)
        def _():
            coupling(c1, c1h, hop)

        put(pa, mm(x, c1))
        put(pb, mm(c1h, x))
        have(b_k, 5)
        have(b_kp, 6)
        have(b_g1, 1)
        put(w1, mm(b_g1, b_k))
        put(w1p, mm(b_kp, b_g1))
        put(f, mm(pa, w1))
        put(fp, mm(w1p, pb))
        put(k, mm(pa, b_g1))
        put(kp, mm(b_g1, pb))
        put(base, plus(x, mm(k, pb)))
        have(b_z, 8)
        put(y, mm(b_z, fp))
        put(g, plus(base, mm(f, y)))

        @pl.when(left)
        def _():
            put(u, mm(v, g))
            put(w, mm(g, t))

        @pl.when(right)
        def _():
            put(u, plus(kp, mm(w1, y)))
            put(r, mm(f, b_z))
            put(w, plus(k, mm(r, w1p)))

    def prepare(g2):
        put(pa, mm(g2, c3))
        put(k, mm(c2, pa))
        put(pb, mm(c3h, g2))
        put(kp, mm(pb, c2h))
        have(b_g1, 1)
        put(w1, mm(b_g1, k))
        put(w1p, mm(kp, b_g1))
        put(pa, plus(c3, mm(c2h, w1)))
        put(f, mm(g2, pa))
        put(pb, plus(c3h, mm(w1p, c2)))
        put(fp, mm(pb, g2))

    @pl.when(place == 2)
    def _():
        @pl.when(left)
        def _():
            coupling(c2, c2h, hop)
            have_raw(3)
            coupling(c3, c3h, raw.at[3])

        @pl.when(right)
        def _():
            coupling(c3, c3h, hop)
            have_raw(2)
            coupling(c2, c2h, raw.at[2])

        prepare(x)
        put(pa, mm(x, c2h))
        put(pb, mm(c2, x))
        put(k, mm(pa, b_g1))
        put(kp, mm(b_g1, pb))
        put(base, plus(x, mm(k, pb)))
        have(b_z, 8)
        put(y, mm(b_z, fp))
        put(g, plus(base, mm(f, y)))
        put(r, mm(f, b_z))

        @pl.when(left)
        def _():
            put(u, plus(kp, mm(w1, y)))
            put(w, plus(k, mm(r, w1p)))

        @pl.when(right)
        def _():
            put(u, (y[0], y[1]))
            put(w, (r[0], r[1]))

    @pl.when(left & (place == 3))
    def _():
        coupling(c3, c3h, hop)
        have_raw(2)
        coupling(c2, c2h, raw.at[2])
        prepare(b_g2)
        have(b_z, 8)
        put(g, (b_z[0], b_z[1]))
        put(u, mm(f, b_z))
        put(w, mm(b_z, fp))

    @pl.when(right & (place == 3))
    def _():
        coupling(c4, c4h, hop)
        have(b_r, 7)
        put(pa, mm(b_r, c4))
        put(pb, mm(c4h, b_r))
        have(b_z, 8)
        put(w, mm(pa, b_z))
        put(g, plus(b_r, mm(w, pb)))
        put(u, mm(b_z, pb))

    spectral[0, 0] = g[0] - g[0].T
    spectral[0, 1] = g[1] + g[1].T
    dr = u[0] - w[0].T
    di = u[1] + w[1].T
    spectral[1, 0] = dr
    spectral[1, 1] = di
    spectral[2, 0] = -dr.T
    spectral[2, 1] = di.T

    def send_d(i, c):
        other = relative(i)
        to_energy(
            spectral.at[:, :, pl.ds(pl.multiple_of(other * 8, 8), 8), :],
            dbuf.at[core, chip], s_d, r_d, other * 2 + core,
        ).start()
        return c

    lax.fori_loop(1, NE // 2, send_d, 0)
    dbuf[core, chip] = spectral[:, :, pl.ds(row, 8), :]
    some = dbuf.at[0, pl.ds(0, NE // 2 - 1)]
    to_energy(some, some, s_d, r_d, e).wait_recv()
    relay = to_energy(dbuf.at[core], dbuf.at[core], s_relay, r_relay, chip * 2 + 1 - core)
    relay.start()
    many = wbuf.at[pl.ds(0, NE - 1)]
    to_energy(many, many, s_w, r_w, e).wait_recv()
    relay.wait_recv()

    def scale(n, c):
        scaled[8 + n] = dbuf[n % 2, n // 2] * factor[n]
        return c

    lax.fori_loop(0, NE, scale, 0)

    def convolve(turn, c):
        start = ((cx + turn) % 4) * 8
        for b in range(3):
            zero = jnp.zeros((8, B), F32)

            def add(k, acc):
                wr, wi = wbuf[k, b, 0], wbuf[k, b, 1]
                new = []
                for i in range(8):
                    lr = scaled[8 + start + i - k, b, 0]
                    li = scaled[8 + start + i - k, b, 1]
                    ar, ai = acc[i]
                    new.append((ar + (lr * wr - li * wi), ai + (lr * wi + li * wr)))
                return tuple(new)

            def add8(k, acc):
                for s in range(8):
                    acc = add(k * 8 + s, acc)
                return acc

            acc = lax.fori_loop(0, start // 8 + 1, add8, tuple((zero, zero) for _ in range(8)))
            for i in range(8):
                sbuf[start + i, b, 0] = -acc[i][1]
                sbuf[start + i, b, 1] = acc[i][0]

        def send_s(i, c2):
            n = start + (i + 2 * cy) % 8

            @pl.when(n != e)
            def _():
                to_energy(
                    sbuf.at[n], out.at[0, 0, core, :, :, pl.ds(row, 8), :], s_sig, r_sig, n
                ).start()

            return c2

        lax.fori_loop(0, 8, send_s, 0)
        return c

    lax.fori_loop(0, 4, convolve, 0)
    out[0, 0, core, :, :, pl.ds(row, 8), :] = sbuf[e]

    for cond, copy in pending:
        pl.when(cond)(copy.wait_send)

    to_energy(many, many, s_w, r_w, e).wait_send()
    to_energy(some, some, s_d, r_d, e).wait_send()
    relay.wait_send()
    to_energy(many, many, s_sig, r_sig, e).wait_send()
    to_energy(many, many, s_sig, r_sig, e).wait_recv()


def local(onsite, hopping, sigma_old, screened):
    vmem = pl.BlockSpec(memory_space=pltpu.VMEM)
    square = pltpu.VMEM((2, B, B), F32)
    return pl.pallas_call(
        kernel,
        out_shape=(
            jax.ShapeDtypeStruct((1, 1, 3, 2, B, B), F32),
            jax.ShapeDtypeStruct((1, 1, 2, 3, 2, B, B), F32),
        ),
        in_specs=[vmem] * 4,
        out_specs=(vmem, vmem),
        scratch_shapes=[pltpu.VMEM((5, 2, B, B), F32)]
        + [square] * 32
        + [
            pltpu.VMEM((3, 2, B, B), F32),
            pltpu.VMEM((NE, 3, 2, 8, B), F32),
            pltpu.VMEM((2, NE // 2, 3, 2, 8, B), F32),
            pltpu.VMEM((NE + 8, 3, 2, 8, B), F32),
            pltpu.VMEM((NE, 8, B), F32),
            pltpu.VMEM((NE, 3, 2, 8, B), F32),
        ]
        + [pltpu.SemaphoreType.DMA((32,))]
        + [pltpu.SemaphoreType.DMA] * 4
        + [pltpu.SemaphoreType.DMA((5,)), pltpu.SemaphoreType.DMA((9,))]
        + [pltpu.SemaphoreType.DMA] * 4,
        compiler_params=pltpu.CompilerParams(
            collective_id=0, has_side_effects=True, vmem_limit_bytes=48 * 2**20
        ),
        name="transport",
    )(onsite, hopping, sigma_old, screened)


def solution(mesh):
    placed = (
        P("space", None, None, None),
        P("space", None, None, None),
        P("energy", "space", None, None, None),
        P("energy", "space", None, None, None, None, None),
    )
    return jax.shard_map(
        local,
        mesh=mesh,
        in_specs=placed,
        out_specs=(
            P("energy", "space", None, None, None, None),
            P("energy", "space", None, None, None, None, None),
        ),
        check_vma=False,
    )
```

```python
import jax
import jax.numpy as jnp
from jax import lax
from jax.experimental import pallas as pl
from jax.experimental.pallas import tpu as pltpu
from jax.sharding import PartitionSpec as P

BROADEN = 0.45
THERMAL = 0.1
B = 128
NE = 32
NC = 8
PANEL = 16
MESH = pl.DeviceIdType.MESH
F32 = jnp.float32


def split(x):
    high = x.astype(jnp.bfloat16)
    return high, (x - high.astype(F32)).astype(jnp.bfloat16)


def dot(a, b):
    return lax.dot_general(a, b, (((1,), (0,)), ((), ())), preferred_element_type=F32)


def product(xr, xi, yr, yi):
    left = jnp.concatenate([xr, xi], axis=1)
    right = jnp.concatenate(
        [jnp.concatenate([yr, yi], axis=1), jnp.concatenate([-yi, yr], axis=1)], axis=0
    )
    lh, ll = split(left)
    rh, rl = split(right)
    out = dot(lh, rh) + (dot(lh, rl) + dot(ll, rh))
    return out[:, :B], out[:, B:]


def mm(x, y):
    return product(x[0], x[1], y[0], y[1])


def put(ref, pair):
    ref[0] = pair[0]
    ref[1] = pair[1]


def put_dagger(ref, x):
    ref[0] = x[0].T
    ref[1] = -x[1].T


def times(a, b):
    return a[0] * b[0] - a[1] * b[1], a[0] * b[1] + a[1] * b[0]


def plus(a, b):
    return a[0] + b[0], a[1] + b[1]


def minus(a, b):
    return a[0] - b[0], a[1] - b[1]


def choose(cond, a, b):
    return jnp.where(cond, a[0], b[0]), jnp.where(cond, a[1], b[1])


def negative(a):
    return -a[0], -a[1]


def tile_inverse(tr, ti, off, lane, sub):
    shape = tr.shape

    def spread(x, k):
        return tuple(jnp.broadcast_to(part[k : k + 1], shape) for part in x)

    cols = [
        tuple(jnp.broadcast_to(part[:, off + j : off + j + 1], shape) for part in (tr, ti))
        for j in range(8)
    ]
    rows = (tr, ti)
    for k in range(0, 8, 2):
        c0, c1 = cols[k], cols[k + 1]
        a, b, c, d = spread(c0, k), spread(c1, k), spread(c0, k + 1), spread(c1, k + 1)
        det = minus(times(a, d), times(b, c))
        own0, own1 = sub == k, sub == k + 1
        either = own0 | own1
        n0 = minus(times(c0, d), times(c1, c))
        n1 = minus(times(c1, a), times(c0, b))
        n0 = choose(own0, negative(d), choose(own1, c, n0))
        n1 = choose(own0, b, choose(own1, negative(a), n1))
        inv = 1.0 / (det[0] * det[0] + det[1] * det[1])
        q = (det[0] * inv, -(det[1] * inv))
        m0, m1 = times(n0, q), times(n1, q)

        def step(x):
            keep = tuple(jnp.where(either, 0.0, part) for part in x)
            return minus(keep, plus(times(m0, spread(x, k)), times(m1, spread(x, k + 1))))

        for j in range(k + 2, 8):
            cols[j] = step(cols[j])
        h0, h1 = lane == off + k, lane == off + k + 1
        unit0, unit1 = jnp.where(own0, 1.0, 0.0), jnp.where(own1, 1.0, 0.0)
        rows = step(
            (
                jnp.where(h0, unit0, jnp.where(h1, unit1, rows[0])),
                jnp.where(h0 | h1, 0.0, rows[1]),
            )
        )
    return rows


def panel_inverse(pr, pi):
    shape = (8, B)
    lane = lax.broadcasted_iota(jnp.int32, shape, 1)
    sub = lax.broadcasted_iota(jnp.int32, shape, 0)
    tiles = [(pr[8 * t : 8 * t + 8], pi[8 * t : 8 * t + 8]) for t in range(PANEL // 8)]
    for t in range(len(tiles)):
        off = 8 * t
        tiles[t] = tile_inverse(*tiles[t], off, lane, sub)
        tr, ti = tiles[t]
        active = (lane >= off) & (lane < off + 8)
        for u in range(len(tiles)):
            if u == t:
                continue
            xr, xi = tiles[u]
            sr, si = jnp.zeros(shape, F32), jnp.zeros(shape, F32)
            for j in range(8):
                cr = jnp.broadcast_to(xr[:, off + j : off + j + 1], shape)
                ci = jnp.broadcast_to(xi[:, off + j : off + j + 1], shape)
                rr = jnp.broadcast_to(tr[j : j + 1], shape)
                ri = jnp.broadcast_to(ti[j : j + 1], shape)
                sr = sr + (cr * rr - ci * ri)
                si = si + (cr * ri + ci * rr)
            tiles[u] = (jnp.where(active, 0.0, xr) - sr, jnp.where(active, 0.0, xi) - si)
    return jnp.concatenate([x[0] for x in tiles]), jnp.concatenate([x[1] for x in tiles])


def invert(x):
    rest = B - PANEL
    lane = lax.broadcasted_iota(jnp.int32, (rest, B), 1)

    def turned(part):
        return pltpu.roll(part, rest, 1)

    def body(_, carry):
        pr, pi, columns, rows = carry
        update = dot(columns, rows)
        xr = x[0, PANEL:, :] - update[:, :B]
        xi = x[1, PANEL:, :] - update[:, B:]
        ch, cl = split(jnp.concatenate([xr[:, :PANEL], xi[:, :PANEL]], axis=1))
        columns = jnp.concatenate([ch, ch, cl], axis=1)
        zr = turned(jnp.where(lane < PANEL, 0.0, xr))
        zi = turned(jnp.where(lane < PANEL, 0.0, xi))
        rr, ri = panel_inverse(pr, pi)
        rr, ri = turned(rr), turned(ri)
        rh, rl = split(
            jnp.concatenate(
                [jnp.concatenate([rr, ri], axis=1), jnp.concatenate([-ri, rr], axis=1)],
                axis=0,
            )
        )
        rows = jnp.concatenate([rh, rl, rh], axis=0)
        new = []
        for t in range(0, PANEL, 8):
            total = (jnp.zeros((8, B), F32), jnp.zeros((8, B), F32))
            for q in range(PANEL):
                col = tuple(
                    jnp.broadcast_to(part[t : t + 8, q : q + 1], (8, B)) for part in (xr, xi)
                )
                row = tuple(jnp.broadcast_to(part[q : q + 1], (8, B)) for part in (rr, ri))
                total = plus(total, times(col, row))
            new.append(minus((zr[t : t + 8], zi[t : t + 8]), total))
        x[0, PANEL:rest, :] = zr[PANEL:]
        x[1, PANEL:rest, :] = zi[PANEL:]
        x[0, rest:, :] = rr
        x[1, rest:, :] = ri
        done = jnp.zeros((PANEL, columns.shape[1]), columns.dtype)
        return (
            jnp.concatenate([part[0] for part in new]),
            jnp.concatenate([part[1] for part in new]),
            jnp.concatenate([columns[PANEL:], done]),
            rows,
        )

    pr, pi, columns, rows = lax.fori_loop(
        0,
        B // PANEL,
        body,
        (
            x[0, :PANEL, :],
            x[1, :PANEL, :],
            jnp.zeros((rest, 6 * PANEL), jnp.bfloat16),
            jnp.zeros((6 * PANEL, 2 * B), jnp.bfloat16),
        ),
    )
    update = dot(columns, rows)
    x[0, PANEL:, :] = x[0, PANEL:, :] - update[:, :B]
    x[1, PANEL:, :] = x[1, PANEL:, :] - update[:, B:]
    x[0, :PANEL, :] = pr
    x[1, :PANEL, :] = pi


def kernel(
    onsite_in, hopping_in, sigma_in, screened, green, out,
    onsite, hop, sigma,
    raw, c1, c1h, c2, c2h, c3, c3h, c4, c4h,
    m, x, r, y, v, t, k, kp, w1, w1p, f, fp, base, pa, pb,
    b_g0, b_g1, b_g2, b_a3, b_mo, b_k, b_kp, b_r, b_z,
    spectral, wbuf, dbuf, scaled, factor, sbuf,
    s_in, s_mat, s_w, s_d, s_relay, s_sig,
    r_raw, r_mat, r_w, r_d, r_relay, r_sig,
):
    e = lax.axis_index("energy")
    j = lax.axis_index("space")
    chip, core = e // 2, e % 2
    cx, cy = chip // 4, chip % 4
    left = j < NC // 2
    right = jnp.logical_not(left)
    place = jnp.where(left, j, NC - 1 - j)
    own = jnp.where(left, j, NC - j)
    row = pl.multiple_of(chip * 8, 8)

    def at(p):
        return jnp.where(left, p, NC - 1 - p)

    def relative(i):
        return ((cx + i // 4) % 4) * 4 + (cy + i % 4) % 4

    loads = [
        pltpu.make_async_copy(onsite_in.at[0], onsite, s_in.at[0]),
        pltpu.make_async_copy(sigma_in.at[0, 0], sigma, s_in.at[1]),
        pltpu.make_async_copy(hopping_in.at[0], hop, s_in.at[2]),
    ]
    for load in loads:
        load.start()
    own_w = pltpu.make_async_copy(
        screened.at[0, 0, core, :, :, pl.ds(row, 8), :], wbuf.at[e], s_in.at[3]
    )
    own_w.start()
    barrier = pltpu.get_barrier_semaphore()

    def greet_z(i, c):
        pl.semaphore_signal(
            barrier, inc=1, device_id={"space": (j + i) % NC}, device_id_type=MESH
        )
        return c

    def greet(i, c):
        pl.semaphore_signal(
            barrier, inc=1, device_id={"energy": (e + i) % NE}, device_id_type=MESH
        )
        return c

    lax.fori_loop(1, NC, greet_z, 0)
    lax.fori_loop(1, NE, greet, 0)

    def energy_of(n, shape):
        return -1.5 + 3.0 * (jnp.full(shape, n, jnp.int32).astype(F32) + 0.5) / NE

    eye = lax.broadcasted_iota(jnp.int32, (B, B), 0) == lax.broadcasted_iota(
        jnp.int32, (B, B), 1
    )
    en = energy_of(e, (B, B))
    for load in loads:
        load.wait()
    on_r, on_i = onsite[0], onsite[1]
    m[0] = jnp.where(eye, en, 0.0) - 0.5 * (on_r + on_r.T) - sigma[0]
    m[1] = jnp.where(eye, BROADEN, 0.0) - 0.5 * (on_i - on_i.T) - sigma[1]
    g, u, w = green.at[0, 0, 0], green.at[0, 0, 1], green.at[0, 0, 2]
    first = (place == 0) | (place == 2)

    def to_space(src, dst, s, r, where):
        return pltpu.make_async_remote_copy(
            src_ref=src, dst_ref=dst, send_sem=s, recv_sem=r,
            device_id={"space": where}, device_id_type=MESH,
        )

    def to_energy(src, dst, s, r, where):
        return pltpu.make_async_remote_copy(
            src_ref=src, dst_ref=dst, send_sem=s, recv_sem=r,
            device_id={"energy": where}, device_id_type=MESH,
        )

    pending = []

    def send(cond, src, dst, sem, where):
        copy = to_space(src, dst, s_mat.at[len(pending)], r_mat.at[sem], where)
        pending.append((cond, copy))
        pl.when(cond)(copy.start)

    def send_raw(cond, src, slot, where):
        copy = to_space(src, raw.at[slot], s_mat.at[len(pending)], r_raw.at[slot], where)
        pending.append((cond, copy))
        pl.when(cond)(copy.start)

    def have(ref, sem):
        to_space(ref, ref, s_mat.at[0], r_mat.at[sem], j).wait_recv()

    def have_raw(slot):
        ref = raw.at[slot]
        to_space(ref, ref, s_mat.at[0], r_raw.at[slot], j).wait_recv()

    def coupling(c, ch, x):
        xr, xi = x[0], x[1]
        dr, di = xr.T, -xi.T
        put(c, (jnp.where(left, xr, dr), jnp.where(left, xi, di)))
        put(ch, (jnp.where(left, dr, xr), jnp.where(left, di, xi)))

    pl.semaphore_wait(barrier, NE - 1 + NC - 1)

    send_raw(left & (place == 1), hop, 1, 0)
    send_raw(left & (place == 2), hop, 2, 1)
    send_raw(left & (place == 3), hop, 3, 1)
    send_raw(right & (place == 0), hop, 1, NC - 2)
    send_raw(right & (place == 1), hop, 2, NC - 3)
    send_raw(right & (place == 2), hop, 3, NC - 2)
    send_raw(left & (place == 2), hop, 2, 3)
    send_raw(left & (place == 3), hop, 3, 2)
    send_raw(right & (place == 3), hop, 4, 3)

    @pl.when(left & (place == 0))
    def _():
        size = en * en + BROADEN * BROADEN
        zr, zi = en / size, -BROADEN / size
        hr, hi = hop[0], hop[1]
        put(v, (zr * hr - zi * hi, zr * hi + zi * hr))
        hr, hi = hop[0].T, -hop[1].T
        put(t, (zr * hr - zi * hi, zr * hi + zi * hr))
        put(m, minus(m, mm(t, hop)))

    @pl.when(first)
    def _():
        x[...] = m[...]
        invert(x)

    send(place == 0, x, b_g0, 0, at(1))
    send(place == 2, x, b_g2, 2, at(1))
    send(place == 2, x, b_g2, 2, at(3))

    def send_w(i, c):
        other = relative(i // 2)
        kind = (core + i % 2) % 2
        to_energy(
            screened.at[0, 0, kind, :, :, pl.ds(pl.multiple_of(other * 8, 8), 8), :],
            wbuf.at[e], s_w, r_w, other * 2 + kind,
        ).start()
        return c

    lax.fori_loop(1, NE, send_w, 0)

    def occupations(n, c):
        f = 1.0 / (1.0 + jnp.exp(energy_of(n, (8, B)) / THERMAL))
        factor[n] = jnp.where(jnp.full((8, B), core, jnp.int32) == 0, -f, 1.0 - f)
        return c

    @pl.when(place != 1)
    def _():
        lax.fori_loop(0, NE, occupations, 0)
        for n in range(8):
            scaled[n] = jnp.zeros_like(scaled[n])

    @pl.when(place == 3)
    def _():
        have(b_g2, 2)

    @pl.when(left & (place == 3))
    def _():
        have_raw(4)

    send(place == 3, m, b_a3, 3, at(1))
    send_raw(left & (place == 3), raw.at[4], 4, 1)
    send_raw(right & (place == 3), hop, 4, NC - 2)

    @pl.when(place == 1)
    def _():
        @pl.when(left)
        def _():
            coupling(c1, c1h, hop)
            have_raw(2)
            coupling(c2, c2h, raw.at[2])

        @pl.when(right)
        def _():
            coupling(c2, c2h, hop)
            have_raw(1)
            coupling(c1, c1h, raw.at[1])

        lax.fori_loop(0, NE, occupations, 0)
        for n in range(8):
            scaled[n] = jnp.zeros_like(scaled[n])
        have_raw(3)
        coupling(c3, c3h, raw.at[3])
        have(b_g2, 2)
        put(pa, mm(b_g2, c3))
        put(k, mm(c2, pa))
        put(kp, mm(c3h, b_g2))
        put(kp, mm(kp, c2h))
        put(base, mm(c3h, pa))
        put(pb, mm(c2, b_g2))
        put(m, minus(m, mm(pb, c2h)))
        have(b_g0, 0)
        put(t, mm(c1h, b_g0))
        put(m, minus(m, mm(t, c1)))

    send(place == 1, k, b_k, 5, at(0))
    send(place == 1, kp, b_kp, 6, at(0))

    @pl.when(place == 1)
    def _():
        x[...] = m[...]
        invert(x)
        put(w1, mm(x, k))
        put(y, mm(kp, w1))
        have(b_a3, 3)
        put(r, minus(minus(b_a3, base), y))
        m[...] = r[...]

    send(place == 1, m, b_mo, 4, NC - 1 - j)
    send(place == 1, x, b_g1, 1, at(2))
    send(left & (place == 1), x, b_g1, 1, 3)
    send(place == 1, x, b_g1, 1, at(0))

    @pl.when(place == 1)
    def _():
        have_raw(4)
        coupling(c4, c4h, raw.at[4])
        invert(r)

    send(right & (place == 1), r, b_r, 7, NC // 2)

    @pl.when(place == 1)
    def _():
        put(pa, mm(r, c4))
        put(pb, mm(c4h, pa))
        put(base, mm(c4h, r))
        have(b_mo, 4)
        put(y, minus(b_mo, pb))
        invert(y)

    send(right & (place == 1), y, b_z, 8, NC // 2)

    @pl.when(place == 1)
    def _():
        put(pb, mm(pa, y))
        put(b_z, plus(r, mm(pb, base)))

    send(place == 1, b_z, b_z, 8, at(2))
    send(left & (place == 1), b_z, b_z, 8, 3)
    send(place == 1, b_z, b_z, 8, at(0))

    @pl.when(place == 1)
    def _():
        put(w1p, mm(kp, x))
        put(f, mm(w1, b_z))
        put(g, plus(x, mm(f, w1p)))

        @pl.when(left)
        def _():
            put(v, mm(b_g0, c1))
            put(u, mm(v, g))
            put(w, mm(g, t))

        @pl.when(right)
        def _():
            put(pa, mm(b_z, w1p))
            put(pa, plus(mm(c2h, g), mm(c3, pa)))
            put(u, mm(b_g2, pa))
            put(pb, plus(mm(g, c2), mm(f, c3h)))
            put(w, mm(pb, b_g2))

    @pl.when(place == 0)
    def _():
        @pl.when(left)
        def _():
            have_raw(1)
            coupling(c1, c1h, raw.at[1])

        @pl.when(right)
        def _():
            coupling(c1, c1h, hop)

        put(pa, mm(x, c1))
        put(pb, mm(c1h, x))
        have(b_k, 5)
        have(b_kp, 6)
        have(b_g1, 1)
        put(w1, mm(b_g1, b_k))
        put(w1p, mm(b_kp, b_g1))
        put(f, mm(pa, w1))
        put(fp, mm(w1p, pb))
        put(k, mm(pa, b_g1))
        put(kp, mm(b_g1, pb))
        put(base, plus(x, mm(k, pb)))

        @pl.when(left)
        def _():
            put(c2, mm(v, base))
            put(c2h, mm(v, f))
            put(c3, mm(base, t))
            put(c3h, mm(fp, t))
            have(b_z, 8)
            put(y, mm(b_z, fp))
            put(r, mm(b_z, c3h))
            put(g, plus(base, mm(f, y)))
            put(u, plus(c2, mm(c2h, y)))
            put(w, plus(c3, mm(f, r)))

        @pl.when(right)
        def _():
            have(b_z, 8)
            put(y, mm(b_z, fp))
            put(g, plus(base, mm(f, y)))
            put(u, plus(kp, mm(w1, y)))
            put(r, mm(f, b_z))
            put(w, plus(k, mm(r, w1p)))

    def prepare(g2):
        put(pa, mm(g2, c3))
        put(k, mm(c2, pa))
        put(pb, mm(c3h, g2))
        put(kp, mm(pb, c2h))
        have(b_g1, 1)
        put(w1, mm(b_g1, k))
        put(w1p, mm(kp, b_g1))
        put(pa, plus(c3, mm(c2h, w1)))
        put(f, mm(g2, pa))
        put(pb, plus(c3h, mm(w1p, c2)))
        put(fp, mm(pb, g2))

    @pl.when(place == 2)
    def _():
        @pl.when(left)
        def _():
            coupling(c2, c2h, hop)
            have_raw(3)
            coupling(c3, c3h, raw.at[3])

        @pl.when(right)
        def _():
            coupling(c3, c3h, hop)
            have_raw(2)
            coupling(c2, c2h, raw.at[2])

        prepare(x)
        put(pa, mm(x, c2h))
        put(pb, mm(c2, x))
        put(k, mm(pa, b_g1))
        put(kp, mm(b_g1, pb))
        put(base, plus(x, mm(k, pb)))
        have(b_z, 8)
        put(y, mm(b_z, fp))
        put(g, plus(base, mm(f, y)))
        put(r, mm(f, b_z))

        @pl.when(left)
        def _():
            put(u, plus(kp, mm(w1, y)))
            put(w, plus(k, mm(r, w1p)))

        @pl.when(right)
        def _():
            put(u, (y[0], y[1]))
            put(w, (r[0], r[1]))

    @pl.when(left & (place == 3))
    def _():
        coupling(c3, c3h, hop)
        have_raw(2)
        coupling(c2, c2h, raw.at[2])
        prepare(b_g2)
        have(b_z, 8)
        put(g, (b_z[0], b_z[1]))
        put(u, mm(f, b_z))
        put(w, mm(b_z, fp))

    @pl.when(right & (place == 3))
    def _():
        coupling(c4, c4h, hop)
        have(b_r, 7)
        put(pa, mm(b_r, c4))
        put(pb, mm(c4h, b_r))
        have(b_z, 8)
        put(w, mm(pa, b_z))
        put(g, plus(b_r, mm(w, pb)))
        put(u, mm(b_z, pb))

    spectral[0, 0] = g[0] - g[0].T
    spectral[0, 1] = g[1] + g[1].T
    dr = u[0] - w[0].T
    di = u[1] + w[1].T
    spectral[1, 0] = dr
    spectral[1, 1] = di
    spectral[2, 0] = -dr.T
    spectral[2, 1] = di.T

    near = sorted(range(1, NE // 2), key=lambda i: min(i // 4, 4 - i // 4) + min(i % 4, 4 - i % 4))
    for i in near[::-1]:
        other = relative(i)
        to_energy(
            spectral.at[:, :, pl.ds(pl.multiple_of(other * 8, 8), 8), :],
            dbuf.at[core, chip], s_d, r_d.at[i], other * 2 + core,
        ).start()
    dbuf[core, chip] = spectral[:, :, pl.ds(row, 8), :]
    sibling = chip * 2 + 1 - core

    def pass_on(source):
        piece = dbuf.at[core, source]
        to_energy(piece, piece, s_relay, r_relay, sibling).start()

    for i in near:
        source = ((cx + 4 - i // 4) % 4) * 4 + (cy + 4 - i % 4) % 4
        piece = dbuf.at[core, source]
        to_energy(piece, piece, s_d, r_d.at[i], e).wait_recv()
        pass_on(source)
    pass_on(chip)
    some = dbuf.at[0, pl.ds(0, NE // 2 - 1)]
    relay = to_energy(dbuf.at[0], dbuf.at[0], s_relay, r_relay, sibling)
    many = wbuf.at[pl.ds(0, NE - 1)]
    own_w.wait()
    to_energy(many, many, s_w, r_w, e).wait_recv()
    relay.wait_recv()

    def scale(n, c):
        scaled[8 + n] = dbuf[n % 2, n // 2] * factor[n]
        return c

    lax.fori_loop(0, NE, scale, 0)

    def convolve(turn, c):
        start = ((cx + turn) % 4) * 8
        for b in range(3):
            zero = jnp.zeros((8, B), F32)

            def add(k, acc):
                wr, wi = wbuf[k, b, 0], wbuf[k, b, 1]
                new = []
                for i in range(8):
                    lr = scaled[8 + start + i - k, b, 0]
                    li = scaled[8 + start + i - k, b, 1]
                    ar, ai = acc[i]
                    new.append((ar + (lr * wr - li * wi), ai + (lr * wi + li * wr)))
                return tuple(new)

            def add8(k, acc):
                for s in range(8):
                    acc = add(k * 8 + s, acc)
                return acc

            acc = lax.fori_loop(0, start // 8 + 1, add8, tuple((zero, zero) for _ in range(8)))
            for i in range(8):
                sbuf[start + i, b, 0] = -acc[i][1]
                sbuf[start + i, b, 1] = acc[i][0]

        def send_s(i, c2):
            n = start + (i + 2 * cy) % 8

            @pl.when(n != e)
            def _():
                to_energy(
                    sbuf.at[n], out.at[0, 0, core, :, :, pl.ds(row, 8), :], s_sig, r_sig, n
                ).start()

            return c2

        lax.fori_loop(0, 8, send_s, 0)
        return c

    lax.fori_loop(0, 4, convolve, 0)
    out[0, 0, core, :, :, pl.ds(row, 8), :] = sbuf[e]

    for cond, copy in pending:
        pl.when(cond)(copy.wait_send)

    to_energy(many, many, s_w, r_w, e).wait_send()
    to_energy(some, some, s_d, r_d.at[0], e).wait_send()
    relay.wait_send()
    to_energy(many, many, s_sig, r_sig, e).wait_send()
    to_energy(many, many, s_sig, r_sig, e).wait_recv()


def local(onsite, hopping, sigma_old, screened):
    vmem = pl.BlockSpec(memory_space=pltpu.VMEM)
    hbm = pl.BlockSpec(memory_space=pltpu.HBM)
    square = pltpu.VMEM((2, B, B), F32)
    return pl.pallas_call(
        kernel,
        out_shape=(
            jax.ShapeDtypeStruct((1, 1, 3, 2, B, B), F32),
            jax.ShapeDtypeStruct((1, 1, 2, 3, 2, B, B), F32),
        ),
        in_specs=[hbm] * 4,
        out_specs=(vmem, vmem),
        scratch_shapes=[square] * 3
        + [pltpu.VMEM((5, 2, B, B), F32)]
        + [square] * 32
        + [
            pltpu.VMEM((3, 2, B, B), F32),
            pltpu.VMEM((NE, 3, 2, 8, B), F32),
            pltpu.VMEM((2, NE // 2, 3, 2, 8, B), F32),
            pltpu.VMEM((NE + 8, 3, 2, 8, B), F32),
            pltpu.VMEM((NE, 8, B), F32),
            pltpu.VMEM((NE, 3, 2, 8, B), F32),
        ]
        + [pltpu.SemaphoreType.DMA((4,)), pltpu.SemaphoreType.DMA((32,))]
        + [pltpu.SemaphoreType.DMA] * 4
        + [pltpu.SemaphoreType.DMA((5,)), pltpu.SemaphoreType.DMA((9,))]
        + [pltpu.SemaphoreType.DMA, pltpu.SemaphoreType.DMA((NE // 2,))]
        + [pltpu.SemaphoreType.DMA] * 2,
        compiler_params=pltpu.CompilerParams(
            collective_id=0, has_side_effects=True, vmem_limit_bytes=48 * 2**20
        ),
        name="transport",
    )(*(pltpu.with_memory_space_constraint(a, pltpu.HBM) for a in (onsite, hopping, sigma_old, screened)))


def solution(mesh):
    placed = (
        P("space", None, None, None),
        P("space", None, None, None),
        P("energy", "space", None, None, None),
        P("energy", "space", None, None, None, None, None),
    )
    return jax.shard_map(
        local,
        mesh=mesh,
        in_specs=placed,
        out_specs=(
            P("energy", "space", None, None, None, None),
            P("energy", "space", None, None, None, None, None),
        ),
        check_vma=False,
    )
```

```python
import jax
import jax.numpy as jnp
from jax import lax
from jax.experimental import pallas as pl
from jax.experimental.pallas import tpu as pltpu
from jax.sharding import PartitionSpec as P

BROADEN = 0.45
THERMAL = 0.1
B = 128
NE = 32
NC = 8
PANEL = 16
MESH = pl.DeviceIdType.MESH
F32 = jnp.float32


def split(x):
    high = x.astype(jnp.bfloat16)
    return high, (x - high.astype(F32)).astype(jnp.bfloat16)


def dot(a, b):
    return lax.dot_general(a, b, (((1,), (0,)), ((), ())), preferred_element_type=F32)


def product(xr, xi, yr, yi):
    left = jnp.concatenate([xr, xi], axis=1)
    right = jnp.concatenate(
        [jnp.concatenate([yr, yi], axis=1), jnp.concatenate([-yi, yr], axis=1)], axis=0
    )
    lh, ll = split(left)
    rh, rl = split(right)
    out = dot(lh, rh) + (dot(lh, rl) + dot(ll, rh))
    return out[:, :B], out[:, B:]


def mm(x, y):
    return product(x[0], x[1], y[0], y[1])


def put(ref, pair):
    ref[0] = pair[0]
    ref[1] = pair[1]


def put_dagger(ref, x):
    ref[0] = x[0].T
    ref[1] = -x[1].T


def times(a, b):
    return a[0] * b[0] - a[1] * b[1], a[0] * b[1] + a[1] * b[0]


def plus(a, b):
    return a[0] + b[0], a[1] + b[1]


def minus(a, b):
    return a[0] - b[0], a[1] - b[1]


def choose(cond, a, b):
    return jnp.where(cond, a[0], b[0]), jnp.where(cond, a[1], b[1])


def negative(a):
    return -a[0], -a[1]


def tile_inverse(tr, ti, off, lane, sub):
    shape = tr.shape

    def spread(x, k):
        return tuple(jnp.broadcast_to(part[k : k + 1], shape) for part in x)

    cols = [
        tuple(jnp.broadcast_to(part[:, off + j : off + j + 1], shape) for part in (tr, ti))
        for j in range(8)
    ]
    rows = (tr, ti)
    for k in range(0, 8, 2):
        c0, c1 = cols[k], cols[k + 1]
        a, b, c, d = spread(c0, k), spread(c1, k), spread(c0, k + 1), spread(c1, k + 1)
        det = minus(times(a, d), times(b, c))
        own0, own1 = sub == k, sub == k + 1
        either = own0 | own1
        n0 = minus(times(c0, d), times(c1, c))
        n1 = minus(times(c1, a), times(c0, b))
        n0 = choose(own0, negative(d), choose(own1, c, n0))
        n1 = choose(own0, b, choose(own1, negative(a), n1))
        inv = 1.0 / (det[0] * det[0] + det[1] * det[1])
        q = (det[0] * inv, -(det[1] * inv))
        m0, m1 = times(n0, q), times(n1, q)

        def step(x):
            keep = tuple(jnp.where(either, 0.0, part) for part in x)
            return minus(keep, plus(times(m0, spread(x, k)), times(m1, spread(x, k + 1))))

        for j in range(k + 2, 8):
            cols[j] = step(cols[j])
        h0, h1 = lane == off + k, lane == off + k + 1
        unit0, unit1 = jnp.where(own0, 1.0, 0.0), jnp.where(own1, 1.0, 0.0)
        rows = step(
            (
                jnp.where(h0, unit0, jnp.where(h1, unit1, rows[0])),
                jnp.where(h0 | h1, 0.0, rows[1]),
            )
        )
    return rows


def panel_inverse(pr, pi):
    shape = (8, B)
    lane = lax.broadcasted_iota(jnp.int32, shape, 1)
    sub = lax.broadcasted_iota(jnp.int32, shape, 0)
    tiles = [(pr[8 * t : 8 * t + 8], pi[8 * t : 8 * t + 8]) for t in range(PANEL // 8)]
    for t in range(len(tiles)):
        off = 8 * t
        tiles[t] = tile_inverse(*tiles[t], off, lane, sub)
        tr, ti = tiles[t]
        active = (lane >= off) & (lane < off + 8)
        for u in range(len(tiles)):
            if u == t:
                continue
            xr, xi = tiles[u]
            sr, si = jnp.zeros(shape, F32), jnp.zeros(shape, F32)
            for j in range(8):
                cr = jnp.broadcast_to(xr[:, off + j : off + j + 1], shape)
                ci = jnp.broadcast_to(xi[:, off + j : off + j + 1], shape)
                rr = jnp.broadcast_to(tr[j : j + 1], shape)
                ri = jnp.broadcast_to(ti[j : j + 1], shape)
                sr = sr + (cr * rr - ci * ri)
                si = si + (cr * ri + ci * rr)
            tiles[u] = (jnp.where(active, 0.0, xr) - sr, jnp.where(active, 0.0, xi) - si)
    return jnp.concatenate([x[0] for x in tiles]), jnp.concatenate([x[1] for x in tiles])


def invert(x):
    rest = B - PANEL
    lane = lax.broadcasted_iota(jnp.int32, (rest, B), 1)

    def turned(part):
        return pltpu.roll(part, rest, 1)

    def body(_, carry):
        pr, pi, columns, rows = carry
        update = dot(columns, rows)
        xr = x[0, PANEL:, :] - update[:, :B]
        xi = x[1, PANEL:, :] - update[:, B:]
        ch, cl = split(jnp.concatenate([xr[:, :PANEL], xi[:, :PANEL]], axis=1))
        columns = jnp.concatenate([ch, ch, cl], axis=1)
        zr = turned(jnp.where(lane < PANEL, 0.0, xr))
        zi = turned(jnp.where(lane < PANEL, 0.0, xi))
        rr, ri = panel_inverse(pr, pi)
        rr, ri = turned(rr), turned(ri)
        rh, rl = split(
            jnp.concatenate(
                [jnp.concatenate([rr, ri], axis=1), jnp.concatenate([-ri, rr], axis=1)],
                axis=0,
            )
        )
        rows = jnp.concatenate([rh, rl, rh], axis=0)
        new = []
        for t in range(0, PANEL, 8):
            total = (jnp.zeros((8, B), F32), jnp.zeros((8, B), F32))
            for q in range(PANEL):
                col = tuple(
                    jnp.broadcast_to(part[t : t + 8, q : q + 1], (8, B)) for part in (xr, xi)
                )
                row = tuple(jnp.broadcast_to(part[q : q + 1], (8, B)) for part in (rr, ri))
                total = plus(total, times(col, row))
            new.append(minus((zr[t : t + 8], zi[t : t + 8]), total))
        x[0, PANEL:rest, :] = zr[PANEL:]
        x[1, PANEL:rest, :] = zi[PANEL:]
        x[0, rest:, :] = rr
        x[1, rest:, :] = ri
        done = jnp.zeros((PANEL, columns.shape[1]), columns.dtype)
        return (
            jnp.concatenate([part[0] for part in new]),
            jnp.concatenate([part[1] for part in new]),
            jnp.concatenate([columns[PANEL:], done]),
            rows,
        )

    pr, pi, columns, rows = lax.fori_loop(
        0,
        B // PANEL,
        body,
        (
            x[0, :PANEL, :],
            x[1, :PANEL, :],
            jnp.zeros((rest, 6 * PANEL), jnp.bfloat16),
            jnp.zeros((6 * PANEL, 2 * B), jnp.bfloat16),
        ),
    )
    update = dot(columns, rows)
    x[0, PANEL:, :] = x[0, PANEL:, :] - update[:, :B]
    x[1, PANEL:, :] = x[1, PANEL:, :] - update[:, B:]
    x[0, :PANEL, :] = pr
    x[1, :PANEL, :] = pi


def kernel(
    onsite_in, hopping_in, sigma_in, screened, green, out,
    onsite, hop, sigma,
    raw, c1, c1h, c2, c2h, c3, c3h, c4, c4h,
    m, x, r, y, v, t, k, kp, w1, w1p, f, fp, base, pa, pb,
    b_g0, b_g1, b_g2, b_a3, b_mo, b_k, b_kp, b_r, b_z,
    spectral, wbuf, packed, dbuf, scaled, factor, sbuf,
    s_in, s_mat, s_w, s_d, s_sig,
    r_raw, r_mat, r_w, r_d, r_sig,
):
    e = lax.axis_index("energy")
    j = lax.axis_index("space")
    chip, core = e // 2, e % 2
    cx, cy = chip // 4, chip % 4
    left = j < NC // 2
    right = jnp.logical_not(left)
    place = jnp.where(left, j, NC - 1 - j)
    own = jnp.where(left, j, NC - j)

    def at(p):
        return jnp.where(left, p, NC - 1 - p)

    def relative(i):
        return ((cx + i // 4) % 4) * 4 + (cy + i % 4) % 4

    loads = [
        pltpu.make_async_copy(onsite_in.at[0], onsite, s_in.at[0]),
        pltpu.make_async_copy(sigma_in.at[0, 0], sigma, s_in.at[1]),
        pltpu.make_async_copy(hopping_in.at[0], hop, s_in.at[2]),
    ]
    for load in loads:
        load.start()
    own_w = pltpu.make_async_copy(
        screened.at[0, 0, :, :, :, e], wbuf.at[e], s_in.at[3]
    )
    own_w.start()
    barrier = pltpu.get_barrier_semaphore()

    def greet_z(i, c):
        pl.semaphore_signal(
            barrier, inc=1, device_id={"space": (j + i) % NC}, device_id_type=MESH
        )
        return c

    def greet(i, c):
        pl.semaphore_signal(
            barrier, inc=1, device_id={"energy": (e + i) % NE}, device_id_type=MESH
        )
        return c

    lax.fori_loop(1, NC, greet_z, 0)
    lax.fori_loop(1, NE, greet, 0)

    def energy_of(n, shape):
        return -1.5 + 3.0 * (jnp.full(shape, n, jnp.int32).astype(F32) + 0.5) / NE

    eye = lax.broadcasted_iota(jnp.int32, (B, B), 0) == lax.broadcasted_iota(
        jnp.int32, (B, B), 1
    )
    en = energy_of(e, (B, B))
    for load in loads:
        load.wait()
    on_r, on_i = onsite[0], onsite[1]
    m[0] = jnp.where(eye, en, 0.0) - 0.5 * (on_r + on_r.T) - sigma[0]
    m[1] = jnp.where(eye, BROADEN, 0.0) - 0.5 * (on_i - on_i.T) - sigma[1]
    g, u, w = green.at[0, 0, 0], green.at[0, 0, 1], green.at[0, 0, 2]
    first = (place == 0) | (place == 2)

    def to_space(src, dst, s, r, where):
        return pltpu.make_async_remote_copy(
            src_ref=src, dst_ref=dst, send_sem=s, recv_sem=r,
            device_id={"space": where}, device_id_type=MESH,
        )

    def to_energy(src, dst, s, r, where):
        return pltpu.make_async_remote_copy(
            src_ref=src, dst_ref=dst, send_sem=s, recv_sem=r,
            device_id={"energy": where}, device_id_type=MESH,
        )

    pending = []

    def send(cond, src, dst, sem, where):
        copy = to_space(src, dst, s_mat.at[len(pending)], r_mat.at[sem], where)
        pending.append((cond, copy))
        pl.when(cond)(copy.start)

    def send_raw(cond, src, slot, where):
        copy = to_space(src, raw.at[slot], s_mat.at[len(pending)], r_raw.at[slot], where)
        pending.append((cond, copy))
        pl.when(cond)(copy.start)

    def have(ref, sem):
        to_space(ref, ref, s_mat.at[0], r_mat.at[sem], j).wait_recv()

    def have_raw(slot):
        ref = raw.at[slot]
        to_space(ref, ref, s_mat.at[0], r_raw.at[slot], j).wait_recv()

    def coupling(c, ch, x):
        xr, xi = x[0], x[1]
        dr, di = xr.T, -xi.T
        put(c, (jnp.where(left, xr, dr), jnp.where(left, xi, di)))
        put(ch, (jnp.where(left, dr, xr), jnp.where(left, di, xi)))

    pl.semaphore_wait(barrier, NE - 1 + NC - 1)

    send_raw(left & (place == 1), hop, 1, 0)
    send_raw(left & (place == 2), hop, 2, 1)
    send_raw(left & (place == 3), hop, 3, 1)
    send_raw(right & (place == 0), hop, 1, NC - 2)
    send_raw(right & (place == 1), hop, 2, NC - 3)
    send_raw(right & (place == 2), hop, 3, NC - 2)
    send_raw(left & (place == 2), hop, 2, 3)
    send_raw(left & (place == 3), hop, 3, 2)
    send_raw(right & (place == 3), hop, 4, 3)

    @pl.when(left & (place == 0))
    def _():
        size = en * en + BROADEN * BROADEN
        zr, zi = en / size, -BROADEN / size
        hr, hi = hop[0], hop[1]
        put(v, (zr * hr - zi * hi, zr * hi + zi * hr))
        hr, hi = hop[0].T, -hop[1].T
        put(t, (zr * hr - zi * hi, zr * hi + zi * hr))
        put(m, minus(m, mm(t, hop)))

    @pl.when(first)
    def _():
        x[...] = m[...]
        invert(x)

    send(place == 0, x, b_g0, 0, at(1))
    send(place == 2, x, b_g2, 2, at(1))
    send(place == 2, x, b_g2, 2, at(3))

    def send_w(i, c):
        other = relative(i // 2) * 2 + (core + i % 2) % 2
        to_energy(
            screened.at[0, 0, :, :, :, other], wbuf.at[e], s_w, r_w, other
        ).start()
        return c

    lax.fori_loop(1, NE, send_w, 0)

    def occupations(n, c):
        f = 1.0 / (1.0 + jnp.exp(energy_of(n, (8, B)) / THERMAL))
        factor[n] = jnp.where(lax.broadcasted_iota(jnp.int32, (8, B), 0) < 4, -f, 1.0 - f)
        return c

    @pl.when(place != 1)
    def _():
        lax.fori_loop(0, NE, occupations, 0)
        for n in range(8):
            scaled[n] = jnp.zeros_like(scaled[n])

    @pl.when(place == 3)
    def _():
        have(b_g2, 2)

    @pl.when(left & (place == 3))
    def _():
        have_raw(4)

    send(place == 3, m, b_a3, 3, at(1))
    send_raw(left & (place == 3), raw.at[4], 4, 1)
    send_raw(right & (place == 3), hop, 4, NC - 2)

    @pl.when(place == 1)
    def _():
        @pl.when(left)
        def _():
            coupling(c1, c1h, hop)
            have_raw(2)
            coupling(c2, c2h, raw.at[2])

        @pl.when(right)
        def _():
            coupling(c2, c2h, hop)
            have_raw(1)
            coupling(c1, c1h, raw.at[1])

        lax.fori_loop(0, NE, occupations, 0)
        for n in range(8):
            scaled[n] = jnp.zeros_like(scaled[n])
        have_raw(3)
        coupling(c3, c3h, raw.at[3])
        have(b_g2, 2)
        put(pa, mm(b_g2, c3))
        put(k, mm(c2, pa))
        put(kp, mm(c3h, b_g2))
        put(kp, mm(kp, c2h))
        put(base, mm(c3h, pa))
        put(pb, mm(c2, b_g2))
        put(m, minus(m, mm(pb, c2h)))
        have(b_g0, 0)
        put(t, mm(c1h, b_g0))
        put(m, minus(m, mm(t, c1)))

    send(place == 1, k, b_k, 5, at(0))
    send(place == 1, kp, b_kp, 6, at(0))

    @pl.when(place == 1)
    def _():
        x[...] = m[...]
        invert(x)
        put(w1, mm(x, k))
        put(y, mm(kp, w1))
        have(b_a3, 3)
        put(r, minus(minus(b_a3, base), y))
        m[...] = r[...]

    send(place == 1, m, b_mo, 4, NC - 1 - j)
    send(place == 1, x, b_g1, 1, at(2))
    send(left & (place == 1), x, b_g1, 1, 3)
    send(place == 1, x, b_g1, 1, at(0))

    @pl.when(place == 1)
    def _():
        have_raw(4)
        coupling(c4, c4h, raw.at[4])
        invert(r)

    send(right & (place == 1), r, b_r, 7, NC // 2)

    @pl.when(place == 1)
    def _():
        put(pa, mm(r, c4))
        put(pb, mm(c4h, pa))
        put(base, mm(c4h, r))
        have(b_mo, 4)
        put(y, minus(b_mo, pb))
        invert(y)

    send(right & (place == 1), y, b_z, 8, NC // 2)

    @pl.when(place == 1)
    def _():
        put(pb, mm(pa, y))
        put(b_z, plus(r, mm(pb, base)))

    send(place == 1, b_z, b_z, 8, at(2))
    send(left & (place == 1), b_z, b_z, 8, 3)
    send(place == 1, b_z, b_z, 8, at(0))

    @pl.when(place == 1)
    def _():
        put(w1p, mm(kp, x))
        put(f, mm(w1, b_z))
        put(g, plus(x, mm(f, w1p)))

        @pl.when(left)
        def _():
            put(v, mm(b_g0, c1))
            put(u, mm(v, g))
            put(w, mm(g, t))

        @pl.when(right)
        def _():
            put(pa, mm(b_z, w1p))
            put(pa, plus(mm(c2h, g), mm(c3, pa)))
            put(u, mm(b_g2, pa))
            put(pb, plus(mm(g, c2), mm(f, c3h)))
            put(w, mm(pb, b_g2))

    @pl.when(place == 0)
    def _():
        @pl.when(left)
        def _():
            have_raw(1)
            coupling(c1, c1h, raw.at[1])

        @pl.when(right)
        def _():
            coupling(c1, c1h, hop)

        put(pa, mm(x, c1))
        put(pb, mm(c1h, x))
        have(b_k, 5)
        have(b_kp, 6)
        have(b_g1, 1)
        put(w1, mm(b_g1, b_k))
        put(w1p, mm(b_kp, b_g1))
        put(f, mm(pa, w1))
        put(fp, mm(w1p, pb))
        put(k, mm(pa, b_g1))
        put(kp, mm(b_g1, pb))
        put(base, plus(x, mm(k, pb)))

        @pl.when(left)
        def _():
            put(c2, mm(v, base))
            put(c2h, mm(v, f))
            put(c3, mm(base, t))
            put(c3h, mm(fp, t))
            have(b_z, 8)
            put(y, mm(b_z, fp))
            put(r, mm(b_z, c3h))
            put(g, plus(base, mm(f, y)))
            put(u, plus(c2, mm(c2h, y)))
            put(w, plus(c3, mm(f, r)))

        @pl.when(right)
        def _():
            have(b_z, 8)
            put(y, mm(b_z, fp))
            put(g, plus(base, mm(f, y)))
            put(u, plus(kp, mm(w1, y)))
            put(r, mm(f, b_z))
            put(w, plus(k, mm(r, w1p)))

    def prepare(g2):
        put(pa, mm(g2, c3))
        put(k, mm(c2, pa))
        put(pb, mm(c3h, g2))
        put(kp, mm(pb, c2h))
        have(b_g1, 1)
        put(w1, mm(b_g1, k))
        put(w1p, mm(kp, b_g1))
        put(pa, plus(c3, mm(c2h, w1)))
        put(f, mm(g2, pa))
        put(pb, plus(c3h, mm(w1p, c2)))
        put(fp, mm(pb, g2))

    @pl.when(place == 2)
    def _():
        @pl.when(left)
        def _():
            coupling(c2, c2h, hop)
            have_raw(3)
            coupling(c3, c3h, raw.at[3])

        @pl.when(right)
        def _():
            coupling(c3, c3h, hop)
            have_raw(2)
            coupling(c2, c2h, raw.at[2])

        prepare(x)
        put(pa, mm(x, c2h))
        put(pb, mm(c2, x))
        put(k, mm(pa, b_g1))
        put(kp, mm(b_g1, pb))
        put(base, plus(x, mm(k, pb)))
        have(b_z, 8)
        put(y, mm(b_z, fp))
        put(g, plus(base, mm(f, y)))
        put(r, mm(f, b_z))

        @pl.when(left)
        def _():
            put(u, plus(kp, mm(w1, y)))
            put(w, plus(k, mm(r, w1p)))

        @pl.when(right)
        def _():
            put(u, (y[0], y[1]))
            put(w, (r[0], r[1]))

    @pl.when(left & (place == 3))
    def _():
        coupling(c3, c3h, hop)
        have_raw(2)
        coupling(c2, c2h, raw.at[2])
        prepare(b_g2)
        have(b_z, 8)
        put(g, (b_z[0], b_z[1]))
        put(u, mm(f, b_z))
        put(w, mm(b_z, fp))

    @pl.when(right & (place == 3))
    def _():
        coupling(c4, c4h, hop)
        have(b_r, 7)
        put(pa, mm(b_r, c4))
        put(pb, mm(c4h, b_r))
        have(b_z, 8)
        put(w, mm(pa, b_z))
        put(g, plus(b_r, mm(w, pb)))
        put(u, mm(b_z, pb))

    dr = u[0] - w[0].T
    di = u[1] + w[1].T
    parts = (
        (g[0] - g[0].T, g[1] + g[1].T),
        (dr, di),
        (-dr.T, di.T),
    )
    for b in range(3):
        for c in range(2):
            for i in range(NE):
                spectral[b, c, i] = parts[b][c][4 * i : 4 * i + 4, :]

    def hops(i):
        return min(i // 4, 4 - i // 4) + min(i % 4, 4 - i % 4)

    for i in sorted(range(NE // 2), key=hops, reverse=True):
        for other_core in (1 - core, core):
            if i == 0 and other_core is core:
                continue
            other = relative(i) * 2 + other_core
            to_energy(spectral.at[:, :, other], dbuf.at[e], s_d, r_d, other).start()

    dbuf[e] = spectral[:, :, e]
    some = dbuf.at[pl.ds(0, NE - 1)]
    many = wbuf.at[pl.ds(0, NE - 1)]
    own_w.wait()
    to_energy(many, many, s_w, r_w, e).wait_recv()

    def pack(n, c):
        for b in range(3):
            for i in range(2):
                packed[n, b, i] = jnp.concatenate([wbuf[n, 0, b, i], wbuf[n, 1, b, i]])
        return c

    lax.fori_loop(0, NE, pack, 0)
    to_energy(some, some, s_d, r_d, e).wait_recv()

    def scale(n, c):
        for b in range(3):
            for i in range(2):
                one = dbuf[n, b, i]
                scaled[8 + n, b, i] = jnp.concatenate([one, one]) * factor[n]
        return c

    lax.fori_loop(0, NE, scale, 0)

    def far(i):
        return jnp.where(i == 0, 2, jnp.where(i == 3, 0, 2 * i - 1))

    def convolve(turn, c):
        start = ((cx + far(turn)) % 4) * 8
        for b in range(3):
            zero = jnp.zeros((8, B), F32)

            def add(k, acc):
                wr, wi = packed[k, b, 0], packed[k, b, 1]
                new = []
                for i in range(8):
                    lr = scaled[8 + start + i - k, b, 0]
                    li = scaled[8 + start + i - k, b, 1]
                    ar, ai = acc[i]
                    new.append((ar + (lr * wr - li * wi), ai + (lr * wi + li * wr)))
                return tuple(new)

            def add8(k, acc):
                for s in range(8):
                    acc = add(k * 8 + s, acc)
                return acc

            acc = lax.fori_loop(0, start // 8 + 1, add8, tuple((zero, zero) for _ in range(8)))
            for i in range(8):
                for kind in range(2):
                    part = slice(4 * kind, 4 * kind + 4)
                    sbuf[start + i, kind, b, 0] = -acc[i][1][part]
                    sbuf[start + i, kind, b, 1] = acc[i][0][part]

        def send_s(i, c2):
            n = start + ((cy + far(i // 2)) % 4) * 2 + (core + 1 + i) % 2

            @pl.when(n != e)
            def _():
                to_energy(
                    sbuf.at[n], out.at[0, 0, :, :, :, e], s_sig, r_sig, n
                ).start()

            return c2

        lax.fori_loop(0, 8, send_s, 0)
        return c

    lax.fori_loop(0, 4, convolve, 0)
    out[0, 0, :, :, :, e] = sbuf[e]

    for cond, copy in pending:
        pl.when(cond)(copy.wait_send)

    to_energy(many, many, s_w, r_w, e).wait_send()
    to_energy(some, some, s_d, r_d, e).wait_send()
    to_energy(many, many, s_sig, r_sig, e).wait_send()
    to_energy(many, many, s_sig, r_sig, e).wait_recv()


def local(onsite, hopping, sigma_old, screened):
    vmem = pl.BlockSpec(memory_space=pltpu.VMEM)
    hbm = pl.BlockSpec(memory_space=pltpu.HBM)
    square = pltpu.VMEM((2, B, B), F32)
    screened = screened.reshape(1, 1, 2, 3, 2, NE, 4, B)
    green, out = pl.pallas_call(
        kernel,
        out_shape=(
            jax.ShapeDtypeStruct((1, 1, 3, 2, B, B), F32),
            jax.ShapeDtypeStruct((1, 1, 2, 3, 2, NE, 4, B), F32),
        ),
        in_specs=[hbm] * 4,
        out_specs=(vmem, vmem),
        scratch_shapes=[square] * 3
        + [pltpu.VMEM((5, 2, B, B), F32)]
        + [square] * 32
        + [
            pltpu.VMEM((3, 2, NE, 4, B), F32),
            pltpu.VMEM((NE, 2, 3, 2, 4, B), F32),
            pltpu.VMEM((NE, 3, 2, 8, B), F32),
            pltpu.VMEM((NE, 3, 2, 4, B), F32),
            pltpu.VMEM((NE + 8, 3, 2, 8, B), F32),
            pltpu.VMEM((NE, 8, B), F32),
            pltpu.VMEM((NE, 2, 3, 2, 4, B), F32),
        ]
        + [pltpu.SemaphoreType.DMA((4,)), pltpu.SemaphoreType.DMA((32,))]
        + [pltpu.SemaphoreType.DMA] * 3
        + [pltpu.SemaphoreType.DMA((5,)), pltpu.SemaphoreType.DMA((9,))]
        + [pltpu.SemaphoreType.DMA] * 3,
        compiler_params=pltpu.CompilerParams(
            collective_id=0, has_side_effects=True, vmem_limit_bytes=48 * 2**20
        ),
        name="transport",
    )(*(pltpu.with_memory_space_constraint(a, pltpu.HBM) for a in (onsite, hopping, sigma_old, screened)))
    return green, out.reshape(1, 1, 2, 3, 2, B, B)


def solution(mesh):
    placed = (
        P("space", None, None, None),
        P("space", None, None, None),
        P("energy", "space", None, None, None),
        P("energy", "space", None, None, None, None, None),
    )
    return jax.shard_map(
        local,
        mesh=mesh,
        in_specs=placed,
        out_specs=(
            P("energy", "space", None, None, None, None),
            P("energy", "space", None, None, None, None, None),
        ),
        check_vma=False,
    )
```

```python
import jax
import jax.numpy as jnp
from jax import lax
from jax.experimental import pallas as pl
from jax.experimental.pallas import tpu as pltpu
from jax.sharding import PartitionSpec as P

BROADEN = 0.45
THERMAL = 0.1
B = 128
NE = 32
NC = 8
PANEL = 16
MESH = pl.DeviceIdType.MESH
F32 = jnp.float32


def split(x):
    high = x.astype(jnp.bfloat16)
    return high, (x - high.astype(F32)).astype(jnp.bfloat16)


def dot(a, b):
    return lax.dot_general(a, b, (((1,), (0,)), ((), ())), preferred_element_type=F32)


def product(xr, xi, yr, yi):
    left = jnp.concatenate([xr, xi], axis=1)
    right = jnp.concatenate(
        [jnp.concatenate([yr, yi], axis=1), jnp.concatenate([-yi, yr], axis=1)], axis=0
    )
    lh, ll = split(left)
    rh, rl = split(right)
    out = dot(lh, rh) + (dot(lh, rl) + dot(ll, rh))
    return out[:, :B], out[:, B:]


def mm(x, y):
    return product(x[0], x[1], y[0], y[1])


def put(ref, pair):
    ref[0] = pair[0]
    ref[1] = pair[1]


def put_dagger(ref, x):
    ref[0] = x[0].T
    ref[1] = -x[1].T


def times(a, b):
    return a[0] * b[0] - a[1] * b[1], a[0] * b[1] + a[1] * b[0]


def plus(a, b):
    return a[0] + b[0], a[1] + b[1]


def minus(a, b):
    return a[0] - b[0], a[1] - b[1]


def choose(cond, a, b):
    return jnp.where(cond, a[0], b[0]), jnp.where(cond, a[1], b[1])


def negative(a):
    return -a[0], -a[1]


def tile_inverse(tr, ti, off, lane, sub):
    shape = tr.shape

    def spread(x, k):
        return tuple(jnp.broadcast_to(part[k : k + 1], shape) for part in x)

    cols = [
        tuple(jnp.broadcast_to(part[:, off + j : off + j + 1], shape) for part in (tr, ti))
        for j in range(8)
    ]
    rows = (tr, ti)
    for k in range(0, 8, 2):
        c0, c1 = cols[k], cols[k + 1]
        a, b, c, d = spread(c0, k), spread(c1, k), spread(c0, k + 1), spread(c1, k + 1)
        det = minus(times(a, d), times(b, c))
        own0, own1 = sub == k, sub == k + 1
        either = own0 | own1
        n0 = minus(times(c0, d), times(c1, c))
        n1 = minus(times(c1, a), times(c0, b))
        n0 = choose(own0, negative(d), choose(own1, c, n0))
        n1 = choose(own0, b, choose(own1, negative(a), n1))
        inv = 1.0 / (det[0] * det[0] + det[1] * det[1])
        q = (det[0] * inv, -(det[1] * inv))
        m0, m1 = times(n0, q), times(n1, q)

        def step(x):
            keep = tuple(jnp.where(either, 0.0, part) for part in x)
            return minus(keep, plus(times(m0, spread(x, k)), times(m1, spread(x, k + 1))))

        for j in range(k + 2, 8):
            cols[j] = step(cols[j])
        h0, h1 = lane == off + k, lane == off + k + 1
        unit0, unit1 = jnp.where(own0, 1.0, 0.0), jnp.where(own1, 1.0, 0.0)
        rows = step(
            (
                jnp.where(h0, unit0, jnp.where(h1, unit1, rows[0])),
                jnp.where(h0 | h1, 0.0, rows[1]),
            )
        )
    return rows


def panel_inverse(pr, pi):
    shape = (8, B)
    lane = lax.broadcasted_iota(jnp.int32, shape, 1)
    sub = lax.broadcasted_iota(jnp.int32, shape, 0)
    tiles = [(pr[8 * t : 8 * t + 8], pi[8 * t : 8 * t + 8]) for t in range(PANEL // 8)]
    for t in range(len(tiles)):
        off = 8 * t
        tiles[t] = tile_inverse(*tiles[t], off, lane, sub)
        tr, ti = tiles[t]
        active = (lane >= off) & (lane < off + 8)
        for u in range(len(tiles)):
            if u == t:
                continue
            xr, xi = tiles[u]
            sr, si = jnp.zeros(shape, F32), jnp.zeros(shape, F32)
            for j in range(8):
                cr = jnp.broadcast_to(xr[:, off + j : off + j + 1], shape)
                ci = jnp.broadcast_to(xi[:, off + j : off + j + 1], shape)
                rr = jnp.broadcast_to(tr[j : j + 1], shape)
                ri = jnp.broadcast_to(ti[j : j + 1], shape)
                sr = sr + (cr * rr - ci * ri)
                si = si + (cr * ri + ci * rr)
            tiles[u] = (jnp.where(active, 0.0, xr) - sr, jnp.where(active, 0.0, xi) - si)
    return jnp.concatenate([x[0] for x in tiles]), jnp.concatenate([x[1] for x in tiles])


def invert(x):
    rest = B - PANEL
    lane = lax.broadcasted_iota(jnp.int32, (rest, B), 1)

    def turned(part):
        return pltpu.roll(part, rest, 1)

    def body(_, carry):
        pr, pi, columns, rows = carry
        update = dot(columns, rows)
        xr = x[0, PANEL:, :] - update[:, :B]
        xi = x[1, PANEL:, :] - update[:, B:]
        ch, cl = split(jnp.concatenate([xr[:, :PANEL], xi[:, :PANEL]], axis=1))
        columns = jnp.concatenate([ch, ch, cl], axis=1)
        zr = turned(jnp.where(lane < PANEL, 0.0, xr))
        zi = turned(jnp.where(lane < PANEL, 0.0, xi))
        rr, ri = panel_inverse(pr, pi)
        rr, ri = turned(rr), turned(ri)
        rh, rl = split(
            jnp.concatenate(
                [jnp.concatenate([rr, ri], axis=1), jnp.concatenate([-ri, rr], axis=1)],
                axis=0,
            )
        )
        rows = jnp.concatenate([rh, rl, rh], axis=0)
        new = []
        for t in range(0, PANEL, 8):
            total = (jnp.zeros((8, B), F32), jnp.zeros((8, B), F32))
            for q in range(PANEL):
                col = tuple(
                    jnp.broadcast_to(part[t : t + 8, q : q + 1], (8, B)) for part in (xr, xi)
                )
                row = tuple(jnp.broadcast_to(part[q : q + 1], (8, B)) for part in (rr, ri))
                total = plus(total, times(col, row))
            new.append(minus((zr[t : t + 8], zi[t : t + 8]), total))
        x[0, PANEL:rest, :] = zr[PANEL:]
        x[1, PANEL:rest, :] = zi[PANEL:]
        x[0, rest:, :] = rr
        x[1, rest:, :] = ri
        done = jnp.zeros((PANEL, columns.shape[1]), columns.dtype)
        return (
            jnp.concatenate([part[0] for part in new]),
            jnp.concatenate([part[1] for part in new]),
            jnp.concatenate([columns[PANEL:], done]),
            rows,
        )

    pr, pi, columns, rows = lax.fori_loop(
        0,
        B // PANEL,
        body,
        (
            x[0, :PANEL, :],
            x[1, :PANEL, :],
            jnp.zeros((rest, 6 * PANEL), jnp.bfloat16),
            jnp.zeros((6 * PANEL, 2 * B), jnp.bfloat16),
        ),
    )
    update = dot(columns, rows)
    x[0, PANEL:, :] = x[0, PANEL:, :] - update[:, :B]
    x[1, PANEL:, :] = x[1, PANEL:, :] - update[:, B:]
    x[0, :PANEL, :] = pr
    x[1, :PANEL, :] = pi


def kernel(
    onsite_in, hopping_in, sigma_in, screened, green, out,
    onsite, hop, sigma,
    raw, c1, c1h, c2, c2h, c3, c3h, c4, c4h,
    m, x, r, y, v, t, k, kp, w1, w1p, f, fp, base, pa, pb,
    b_g0, b_g1, b_g2, b_a3, b_mo, b_k, b_kp, b_r, b_z,
    spectral, wbuf, packed, dbuf, scaled, factor, sbuf,
    s_in, s_mat, s_w, s_d, s_sig,
    r_raw, r_mat, r_w, r_d, r_sig,
):
    e = lax.axis_index("energy")
    j = lax.axis_index("space")
    chip, core = e // 2, e % 2
    cx, cy = chip // 4, chip % 4
    left = j < NC // 2
    right = jnp.logical_not(left)
    place = jnp.where(left, j, NC - 1 - j)
    own = jnp.where(left, j, NC - j)

    def at(p):
        return jnp.where(left, p, NC - 1 - p)

    def relative(i):
        return ((cx + i // 4) % 4) * 4 + (cy + i % 4) % 4

    loads = [
        pltpu.make_async_copy(onsite_in.at[0], onsite, s_in.at[0]),
        pltpu.make_async_copy(sigma_in.at[0, 0], sigma, s_in.at[1]),
        pltpu.make_async_copy(hopping_in.at[0], hop, s_in.at[2]),
    ]
    for load in loads:
        load.start()
    own_w = pltpu.make_async_copy(
        screened.at[0, 0, :, :, :, e], wbuf.at[e], s_in.at[3]
    )
    own_w.start()
    barrier = pltpu.get_barrier_semaphore()

    def greet_z(i, c):
        pl.semaphore_signal(
            barrier, inc=1, device_id={"space": (j + i) % NC}, device_id_type=MESH
        )
        return c

    def greet(i, c):
        pl.semaphore_signal(
            barrier, inc=1, device_id={"energy": (e + i) % NE}, device_id_type=MESH
        )
        return c

    lax.fori_loop(1, NC, greet_z, 0)
    lax.fori_loop(1, NE, greet, 0)

    def energy_of(n, shape):
        return -1.5 + 3.0 * (jnp.full(shape, n, jnp.int32).astype(F32) + 0.5) / NE

    eye = lax.broadcasted_iota(jnp.int32, (B, B), 0) == lax.broadcasted_iota(
        jnp.int32, (B, B), 1
    )
    en = energy_of(e, (B, B))
    for load in loads:
        load.wait()
    on_r, on_i = onsite[0], onsite[1]
    m[0] = jnp.where(eye, en, 0.0) - 0.5 * (on_r + on_r.T) - sigma[0]
    m[1] = jnp.where(eye, BROADEN, 0.0) - 0.5 * (on_i - on_i.T) - sigma[1]
    g, u, w = green.at[0, 0, 0], green.at[0, 0, 1], green.at[0, 0, 2]
    first = (place == 0) | (place == 2)

    def to_space(src, dst, s, r, where):
        return pltpu.make_async_remote_copy(
            src_ref=src, dst_ref=dst, send_sem=s, recv_sem=r,
            device_id={"space": where}, device_id_type=MESH,
        )

    def to_energy(src, dst, s, r, where):
        return pltpu.make_async_remote_copy(
            src_ref=src, dst_ref=dst, send_sem=s, recv_sem=r,
            device_id={"energy": where}, device_id_type=MESH,
        )

    pending = []

    def send(cond, src, dst, sem, where):
        copy = to_space(src, dst, s_mat.at[len(pending)], r_mat.at[sem], where)
        pending.append((cond, copy))
        pl.when(cond)(copy.start)

    def send_raw(cond, src, slot, where):
        copy = to_space(src, raw.at[slot], s_mat.at[len(pending)], r_raw.at[slot], where)
        pending.append((cond, copy))
        pl.when(cond)(copy.start)

    def have(ref, sem):
        to_space(ref, ref, s_mat.at[0], r_mat.at[sem], j).wait_recv()

    def have_raw(slot):
        ref = raw.at[slot]
        to_space(ref, ref, s_mat.at[0], r_raw.at[slot], j).wait_recv()

    def coupling(c, ch, x):
        xr, xi = x[0], x[1]
        dr, di = xr.T, -xi.T
        put(c, (jnp.where(left, xr, dr), jnp.where(left, xi, di)))
        put(ch, (jnp.where(left, dr, xr), jnp.where(left, di, xi)))

    pl.semaphore_wait(barrier, NE - 1 + NC - 1)

    send_raw(left & (place == 1), hop, 1, 0)
    send_raw(left & (place == 2), hop, 2, 1)
    send_raw(left & (place == 3), hop, 3, 1)
    send_raw(right & (place == 0), hop, 1, NC - 2)
    send_raw(right & (place == 1), hop, 2, NC - 3)
    send_raw(right & (place == 2), hop, 3, NC - 2)
    send_raw(left & (place == 2), hop, 2, 3)
    send_raw(left & (place == 3), hop, 3, 2)
    send_raw(right & (place == 3), hop, 4, 3)

    @pl.when(left & (place == 0))
    def _():
        size = en * en + BROADEN * BROADEN
        zr, zi = en / size, -BROADEN / size
        hr, hi = hop[0], hop[1]
        put(v, (zr * hr - zi * hi, zr * hi + zi * hr))
        hr, hi = hop[0].T, -hop[1].T
        put(t, (zr * hr - zi * hi, zr * hi + zi * hr))
        put(m, minus(m, mm(t, hop)))

    @pl.when(first)
    def _():
        x[...] = m[...]
        invert(x)

    send(place == 0, x, b_g0, 0, at(1))
    send(place == 2, x, b_g2, 2, at(1))
    send(place == 2, x, b_g2, 2, at(3))

    def send_w(i, c):
        other = relative(i // 2) * 2 + (core + i % 2) % 2
        to_energy(
            screened.at[0, 0, :, :, :, other], wbuf.at[e], s_w, r_w, other
        ).start()
        return c

    lax.fori_loop(1, NE, send_w, 0)

    def occupations(n, c):
        f = 1.0 / (1.0 + jnp.exp(energy_of(n, (8, B)) / THERMAL))
        factor[n] = jnp.where(lax.broadcasted_iota(jnp.int32, (8, B), 0) < 4, -f, 1.0 - f)
        return c

    @pl.when(place != 1)
    def _():
        lax.fori_loop(0, NE, occupations, 0)
        for n in range(8):
            scaled[n] = jnp.zeros_like(scaled[n])

    @pl.when(place == 3)
    def _():
        have(b_g2, 2)

    @pl.when(left & (place == 3))
    def _():
        have_raw(4)

    send(place == 3, m, b_a3, 3, at(1))
    send_raw(left & (place == 3), raw.at[4], 4, 1)
    send_raw(right & (place == 3), hop, 4, NC - 2)

    @pl.when(place == 1)
    def _():
        @pl.when(left)
        def _():
            coupling(c1, c1h, hop)
            have_raw(2)
            coupling(c2, c2h, raw.at[2])

        @pl.when(right)
        def _():
            coupling(c2, c2h, hop)
            have_raw(1)
            coupling(c1, c1h, raw.at[1])

        lax.fori_loop(0, NE, occupations, 0)
        for n in range(8):
            scaled[n] = jnp.zeros_like(scaled[n])
        have_raw(3)
        coupling(c3, c3h, raw.at[3])
        have(b_g2, 2)
        put(pa, mm(b_g2, c3))
        put(k, mm(c2, pa))
        put(kp, mm(c3h, b_g2))
        put(kp, mm(kp, c2h))
        put(base, mm(c3h, pa))
        put(pb, mm(c2, b_g2))
        put(m, minus(m, mm(pb, c2h)))
        have(b_g0, 0)
        put(t, mm(c1h, b_g0))
        put(m, minus(m, mm(t, c1)))

    send(place == 1, k, b_k, 5, at(0))
    send(place == 1, kp, b_kp, 6, at(0))

    @pl.when(place == 1)
    def _():
        x[...] = m[...]
        invert(x)
        put(w1, mm(x, k))
        put(y, mm(kp, w1))
        have(b_a3, 3)
        put(r, minus(minus(b_a3, base), y))
        m[...] = r[...]

    send(place == 1, m, b_mo, 4, NC - 1 - j)
    send(place == 1, x, b_g1, 1, at(2))
    send(left & (place == 1), x, b_g1, 1, 3)
    send(place == 1, x, b_g1, 1, at(0))

    @pl.when(place == 1)
    def _():
        have_raw(4)
        coupling(c4, c4h, raw.at[4])
        invert(r)

    send(right & (place == 1), r, b_r, 7, NC // 2)

    @pl.when(place == 1)
    def _():
        put(pa, mm(r, c4))
        put(pb, mm(c4h, pa))
        put(base, mm(c4h, r))
        have(b_mo, 4)
        put(y, minus(b_mo, pb))
        invert(y)

    send(right & (place == 1), y, b_z, 8, NC // 2)

    @pl.when(place == 1)
    def _():
        put(pb, mm(pa, y))
        put(b_z, plus(r, mm(pb, base)))

    send(place == 1, b_z, b_z, 8, at(0))
    send(place == 1, b_z, b_z, 8, at(2))
    send(left & (place == 1), b_z, b_z, 8, 3)

    @pl.when(place == 1)
    def _():
        put(w1p, mm(kp, x))
        put(f, mm(w1, b_z))
        put(g, plus(x, mm(f, w1p)))

        @pl.when(left)
        def _():
            put(v, mm(b_g0, c1))
            put(u, mm(v, g))
            put(w, mm(g, t))

        @pl.when(right)
        def _():
            put(pa, mm(b_z, w1p))
            put(pa, plus(mm(c2h, g), mm(c3, pa)))
            put(u, mm(b_g2, pa))
            put(pb, plus(mm(g, c2), mm(f, c3h)))
            put(w, mm(pb, b_g2))

    @pl.when(place == 0)
    def _():
        @pl.when(left)
        def _():
            have_raw(1)
            coupling(c1, c1h, raw.at[1])

        @pl.when(right)
        def _():
            coupling(c1, c1h, hop)

        put(pa, mm(x, c1))
        put(pb, mm(c1h, x))
        have(b_k, 5)
        have(b_kp, 6)
        have(b_g1, 1)
        put(w1, mm(b_g1, b_k))
        put(w1p, mm(b_kp, b_g1))
        put(f, mm(pa, w1))
        put(fp, mm(w1p, pb))
        put(k, mm(pa, b_g1))
        put(kp, mm(b_g1, pb))
        put(base, plus(x, mm(k, pb)))

        @pl.when(left)
        def _():
            put(c2, mm(v, base))
            put(c2h, mm(v, f))
            put(c3, mm(base, t))
            put(c3h, mm(fp, t))
            have(b_z, 8)
            put(y, mm(b_z, fp))
            put(r, mm(b_z, c3h))
            put(g, plus(base, mm(f, y)))
            put(u, plus(c2, mm(c2h, y)))
            put(w, plus(c3, mm(f, r)))

        @pl.when(right)
        def _():
            have(b_z, 8)
            put(y, mm(b_z, fp))
            put(g, plus(base, mm(f, y)))
            put(u, plus(kp, mm(w1, y)))
            put(r, mm(f, b_z))
            put(w, plus(k, mm(r, w1p)))

    def prepare(g2):
        put(pa, mm(g2, c3))
        put(k, mm(c2, pa))
        put(pb, mm(c3h, g2))
        put(kp, mm(pb, c2h))
        have(b_g1, 1)
        put(w1, mm(b_g1, k))
        put(w1p, mm(kp, b_g1))
        put(pa, plus(c3, mm(c2h, w1)))
        put(f, mm(g2, pa))
        put(pb, plus(c3h, mm(w1p, c2)))
        put(fp, mm(pb, g2))

    @pl.when(place == 2)
    def _():
        @pl.when(left)
        def _():
            coupling(c2, c2h, hop)
            have_raw(3)
            coupling(c3, c3h, raw.at[3])

        @pl.when(right)
        def _():
            coupling(c3, c3h, hop)
            have_raw(2)
            coupling(c2, c2h, raw.at[2])

        prepare(x)
        put(pa, mm(x, c2h))
        put(pb, mm(c2, x))
        put(k, mm(pa, b_g1))
        put(kp, mm(b_g1, pb))
        put(base, plus(x, mm(k, pb)))
        have(b_z, 8)
        put(y, mm(b_z, fp))
        put(g, plus(base, mm(f, y)))
        put(r, mm(f, b_z))

        @pl.when(left)
        def _():
            put(u, plus(kp, mm(w1, y)))
            put(w, plus(k, mm(r, w1p)))

        @pl.when(right)
        def _():
            put(u, (y[0], y[1]))
            put(w, (r[0], r[1]))

    @pl.when(left & (place == 3))
    def _():
        coupling(c3, c3h, hop)
        have_raw(2)
        coupling(c2, c2h, raw.at[2])
        prepare(b_g2)
        have(b_z, 8)
        put(g, (b_z[0], b_z[1]))
        put(u, mm(f, b_z))
        put(w, mm(b_z, fp))

    @pl.when(right & (place == 3))
    def _():
        coupling(c4, c4h, hop)
        have(b_r, 7)
        put(pa, mm(b_r, c4))
        put(pb, mm(c4h, b_r))
        have(b_z, 8)
        put(w, mm(pa, b_z))
        put(g, plus(b_r, mm(w, pb)))
        put(u, mm(b_z, pb))

    dr = u[0] - w[0].T
    di = u[1] + w[1].T
    parts = (
        (g[0] - g[0].T, g[1] + g[1].T),
        (dr, di),
        (-dr.T, di.T),
    )
    for b in range(3):
        for c in range(2):
            for i in range(NE):
                spectral[b, c, i] = parts[b][c][4 * i : 4 * i + 4, :]

    def hops(i):
        return min(i // 4, 4 - i // 4) + min(i % 4, 4 - i % 4)

    for i in sorted(range(NE // 2), key=hops, reverse=True):
        for other_core in (1 - core, core):
            if i == 0 and other_core is core:
                continue
            other = relative(i) * 2 + other_core
            to_energy(spectral.at[:, :, other], dbuf.at[e], s_d, r_d, other).start()

    dbuf[e] = spectral[:, :, e]
    some = dbuf.at[pl.ds(0, NE - 1)]
    many = wbuf.at[pl.ds(0, NE - 1)]
    own_w.wait()
    to_energy(many, many, s_w, r_w, e).wait_recv()

    def pack(n, c):
        for b in range(3):
            for i in range(2):
                packed[n, b, i] = jnp.concatenate([wbuf[n, 0, b, i], wbuf[n, 1, b, i]])
            packed[n, b, 2] = packed[n, b, 0] + packed[n, b, 1]
        return c

    lax.fori_loop(0, NE, pack, 0)
    to_energy(some, some, s_d, r_d, e).wait_recv()

    def scale(n, c):
        for b in range(3):
            for i in range(2):
                one = dbuf[n, b, i]
                scaled[8 + n, b, i] = jnp.concatenate([one, one]) * factor[n]
            scaled[8 + n, b, 2] = scaled[8 + n, b, 0] + scaled[8 + n, b, 1]
        return c

    lax.fori_loop(0, NE, scale, 0)

    def far(i):
        return jnp.where(i == 0, 2, jnp.where(i == 3, 0, 2 * i - 1))

    def convolve(turn, c):
        start = ((cx + far(turn)) % 4) * 8
        for b in range(3):
            zero = jnp.zeros((8, B), F32)

            def add(k, acc):
                wr, wi, ws = packed[k, b, 0], packed[k, b, 1], packed[k, b, 2]
                new = []
                for i in range(8):
                    lr = scaled[8 + start + i - k, b, 0]
                    li = scaled[8 + start + i - k, b, 1]
                    ls = scaled[8 + start + i - k, b, 2]
                    rr, ii, both = acc[i]
                    new.append((rr + lr * wr, ii + li * wi, both + ls * ws))
                return tuple(new)

            def add8(k, acc):
                for s in range(8):
                    acc = add(k * 8 + s, acc)
                return acc

            acc = lax.fori_loop(0, start // 8 + 1, add8, tuple((zero, zero, zero) for _ in range(8)))
            for i in range(8):
                rr, ii, both = acc[i]
                for kind in range(2):
                    part = slice(4 * kind, 4 * kind + 4)
                    sbuf[start + i, kind, b, 0] = (rr + ii - both)[part]
                    sbuf[start + i, kind, b, 1] = (rr - ii)[part]

        def send_s(i, c2):
            n = start + ((cy + far(i // 2)) % 4) * 2 + (core + 1 + i) % 2

            @pl.when(n != e)
            def _():
                to_energy(
                    sbuf.at[n], out.at[0, 0, :, :, :, e], s_sig, r_sig, n
                ).start()

            return c2

        lax.fori_loop(0, 8, send_s, 0)
        return c

    lax.fori_loop(0, 4, convolve, 0)
    out[0, 0, :, :, :, e] = sbuf[e]

    for cond, copy in pending:
        pl.when(cond)(copy.wait_send)

    to_energy(many, many, s_w, r_w, e).wait_send()
    to_energy(some, some, s_d, r_d, e).wait_send()
    to_energy(many, many, s_sig, r_sig, e).wait_send()
    to_energy(many, many, s_sig, r_sig, e).wait_recv()


def local(onsite, hopping, sigma_old, screened):
    vmem = pl.BlockSpec(memory_space=pltpu.VMEM)
    hbm = pl.BlockSpec(memory_space=pltpu.HBM)
    square = pltpu.VMEM((2, B, B), F32)
    screened = screened.reshape(1, 1, 2, 3, 2, NE, 4, B)
    green, out = pl.pallas_call(
        kernel,
        out_shape=(
            jax.ShapeDtypeStruct((1, 1, 3, 2, B, B), F32),
            jax.ShapeDtypeStruct((1, 1, 2, 3, 2, NE, 4, B), F32),
        ),
        in_specs=[hbm] * 4,
        out_specs=(vmem, vmem),
        scratch_shapes=[square] * 3
        + [pltpu.VMEM((5, 2, B, B), F32)]
        + [square] * 32
        + [
            pltpu.VMEM((3, 2, NE, 4, B), F32),
            pltpu.VMEM((NE, 2, 3, 2, 4, B), F32),
            pltpu.VMEM((NE, 3, 3, 8, B), F32),
            pltpu.VMEM((NE, 3, 2, 4, B), F32),
            pltpu.VMEM((NE + 8, 3, 3, 8, B), F32),
            pltpu.VMEM((NE, 8, B), F32),
            pltpu.VMEM((NE, 2, 3, 2, 4, B), F32),
        ]
        + [pltpu.SemaphoreType.DMA((4,)), pltpu.SemaphoreType.DMA((32,))]
        + [pltpu.SemaphoreType.DMA] * 3
        + [pltpu.SemaphoreType.DMA((5,)), pltpu.SemaphoreType.DMA((9,))]
        + [pltpu.SemaphoreType.DMA] * 3,
        compiler_params=pltpu.CompilerParams(
            collective_id=0, has_side_effects=True, vmem_limit_bytes=48 * 2**20
        ),
        name="transport",
    )(*(pltpu.with_memory_space_constraint(a, pltpu.HBM) for a in (onsite, hopping, sigma_old, screened)))
    return green, out.reshape(1, 1, 2, 3, 2, B, B)


def solution(mesh):
    placed = (
        P("space", None, None, None),
        P("space", None, None, None),
        P("energy", "space", None, None, None),
        P("energy", "space", None, None, None, None, None),
    )
    return jax.shard_map(
        local,
        mesh=mesh,
        in_specs=placed,
        out_specs=(
            P("energy", "space", None, None, None, None),
            P("energy", "space", None, None, None, None, None),
        ),
        check_vma=False,
    )
```
